128 devices in a mesh: gx: 8 (over y_lo, z), gy: 16 (over x, y_hi, core).
Axes of the slice: x: 4, y: 4 (y_hi: 2, y_lo: 2; y = y_hi * 2 + y_lo), z: 4, core: 2. Of those that a mesh axis runs over, the one named last changes fastest.
Arguments:
- group_one: bfloat16 [24576, 768], P(('gx', 'gy')), may hold values from -6 to 6
- routes_one: int32 [24576, 1], P(('gx', 'gy')), may hold values from 0 to 127; in each aligned block of 192 rows (0 to 191, 192 to 383, ...) at most 6 rows name the same one
- gates_one: float32 [24576], P(('gx', 'gy')), may hold values from 0.2 to 1
- group_two: bfloat16 [24576, 768], P(('gx', 'gy')), may hold values from -6 to 6
- routes_two: int32 [24576, 1], P(('gx', 'gy')), may hold values from 0 to 127; in each aligned block of 192 rows (0 to 191, 192 to 383, ...) at most 6 rows name the same one
- gates_two: float32 [24576], P(('gx', 'gy')), may hold values from 0.2 to 1
- norm_gain: float32 [768], replicated, may hold values from 0.1 to 1.9
- weight_in: bfloat16 [128, 768, 3072], P(('gx', 'gy')), may hold values from -0.21875 to 0.21875
- weight_out: bfloat16 [128, 3072, 768], P(('gx', 'gy')), may hold values from -0.109375 to 0.109375
- old_place: int32 [128], replicated, may hold values from 0 to 127, each once
- partner: int32 [128], replicated, may hold values from 0 to 127, as said below
Outputs:
- result_one: bfloat16 [24576, 768], P(('gx', 'gy'))
- result_two: bfloat16 [24576, 768], P(('gx', 'gy'))
- new_in: bfloat16 [128, 768, 3072], P(('gx', 'gy'))
- new_out: bfloat16 [128, 3072, 768], P(('gx', 'gy'))
The draws below stay inside these ranges and needn't reach their ends.
Inputs may be any that keep to these rules, and one draw needn't show every extreme that they name: `routes_one`: at most 6 tokens of one device's rows in a block name the same expert, a bound that some block reaches of some device's rows in every draw. `routes_two`: same law as routes_one. partner is an involution: partner[partner[s]] = s; exactly 64 slots have partner[s] != s.
All inputs are finite; a program needn't handle non-finite values.
Results may differ from the reference program's by a relative error of at most 0.0041.
Values may be sent and summed in bfloat16 or wider, within the bound.
No kernel may reach another device: no remote copies, remote signals or barrier semaphores. Data moves between devices by JAX's collectives and lax.ppermute only.
A program may use at most 128 MiB of HBM per device.

```python
import math
import jax
import jax.numpy as jnp
import numpy as np
from jax import lax

D = 768
FF = 3072
TOK_DEV = 192
CAP = 6
EXPERTS = 128
TOKENS = 24576
EXPERT_ROWS = 768


def draw_partner(key, part):
    shuffled = jax.random.permutation(jax.random.fold_in(key, 7), EXPERTS).astype(jnp.int32)
    moved = EXPERTS // 2
    givers = shuffled[0:moved:2]
    takers = shuffled[1:moved:2]
    labels = jnp.arange(EXPERTS, dtype=jnp.int32)
    return labels.at[givers].set(takers).at[takers].set(givers)


def steps_of(stream_key, extent, split, low, top_value):
    factor_of, own = 1.0, jax.random.fold_in(stream_key, 6)
    for dim, blocks in split:
        heights = jnp.exp(jax.random.uniform(jax.random.fold_in(own, dim), (blocks,), jnp.float32, low / len(split), top_value / len(split)))
        factor_of = factor_of * jnp.repeat(heights, extent[dim] // blocks).reshape([-1 if axis == dim else 1 for axis in range(len(extent))])
    return factor_of


def shared_out(own_key, own, number, rows, count, top, limit, slope):
    sequence = jax.random.permutation(own_key, count)
    heavy_load, common = portions_of(count, rows * top, limit, slope, True), portions_of(count, rows * top, limit, slope, False)
    places = jnp.arange(count)

    def named(lengths, offset_by):
        used = int((lengths > 0).sum())
        fixed = max(1, used // 4)
        shifted = fixed + (places - fixed + offset_by * (used - fixed)) % max(1, count - fixed)
        return jnp.zeros((count,), jnp.int32).at[sequence[jnp.where(places < fixed, places, shifted)]].set(jnp.asarray(lengths, jnp.int32))

    lengths = jnp.where(number % 4 == 0, named(heavy_load, number // 4), named(common, number - number // 4 - 1))
    mixed = jax.random.permutation(jax.random.fold_in(own, 3), count)
    giver, taker = mixed[0:count // 2 * 2:2], mixed[1:count // 2 * 2:2]
    margin = jnp.minimum(lengths[giver] - 1, limit - lengths[taker]) // 2
    margin = jnp.where((giver == sequence[0]) | (taker == sequence[0]) | (lengths[taker] == 0), 0, jnp.maximum(margin, 0))
    shifted = jax.random.randint(jax.random.fold_in(own, 4), (count // 2,), 0, 1 << 20) % (margin + 1)
    lengths = lengths.at[giver].add(-shifted).at[taker].add(shifted)
    items = jnp.searchsorted(jnp.cumsum(lengths), jnp.arange(rows * top), side="right").astype(jnp.int32)
    table = items.reshape(top, rows).T
    table = table[jax.random.permutation(jax.random.fold_in(own, 1), rows)]
    offset_by = jax.random.randint(jax.random.fold_in(own, 2), (rows, 1), 0, top)
    return jnp.take_along_axis(table, (jnp.arange(top)[None, :] + offset_by) % top, axis=1)


def portions_of(number_of, total, bound, lean, full):
    weights = [(1 << 20) // math.isqrt(grade ** lean) + 1 for grade in range(1, number_of + 1)]
    largest = bound if full else min(bound, max(-(-total // number_of), total * weights[0] // sum(weights)))
    least = 1 if total - largest >= number_of - 1 else 0
    given, spare = [largest] + [least] * (number_of - 1), total - largest - least * (number_of - 1)
    while spare > 0:
        free = [i for i in range(1, number_of) if given[i] < largest] or [i for i in range(1, number_of) if given[i] < bound]
        whole, remaining = sum([weights[i] for i in free]), spare
        for i in free:
            extra = min(bound - given[i], max(1, remaining * weights[i] // whole), spare)
            given[i] = given[i] + extra
            spare = spare - extra
    return np.array(given)


def centred(rng, extent, width, most, cuts=(), kind=jnp.bfloat16):
    drawn = width * jax.random.normal(rng, extent, jnp.float32)
    if cuts:
        drawn = drawn * steps_of(rng, extent, cuts, -0.22, 0.18)
    return jnp.clip(drawn, -most, most).astype(kind)


def setup_inputs(seed: int = 0) -> dict:
    arg_keys = jax.random.split(jax.random.key(seed), 12)
    group_one = centred(arg_keys[0], (TOKENS, D), 1.0, 6.0, ((0, 128),))
    routes_one_keys = jax.random.split(jax.random.fold_in(arg_keys[1], 1), TOKENS // TOK_DEV)
    routes_one_turns = jax.random.permutation(jax.random.fold_in(arg_keys[1], 3), TOKENS // TOK_DEV)
    routes_one = jax.vmap(lambda own, number: shared_out(jax.random.fold_in(arg_keys[1], 2), own, number, TOK_DEV, EXPERTS, 1, CAP, 2))(routes_one_keys, routes_one_turns).reshape((TOKENS, 1))
    gates_one = jnp.clip(0.2 + 0.8 * jax.random.uniform(arg_keys[2], (TOKENS,), jnp.float32) ** steps_of(arg_keys[2], (TOKENS,), ((0, 128),), -0.2, 0.2), 0.2, 1.0)
    group_two = centred(arg_keys[3], (TOKENS, D), 1.0, 6.0, ((0, 128),))
    routes_two_keys = jax.random.split(jax.random.fold_in(arg_keys[4], 1), TOKENS // TOK_DEV)
    routes_two_turns = jax.random.permutation(jax.random.fold_in(arg_keys[4], 3), TOKENS // TOK_DEV)
    routes_two = jax.vmap(lambda own, number: shared_out(jax.random.fold_in(arg_keys[4], 2), own, number, TOK_DEV, EXPERTS, 1, CAP, 2))(routes_two_keys, routes_two_turns).reshape((TOKENS, 1))
    gates_two = jnp.clip(0.2 + 0.8 * jax.random.uniform(arg_keys[5], (TOKENS,), jnp.float32) ** steps_of(arg_keys[5], (TOKENS,), ((0, 128),), -0.2, 0.2), 0.2, 1.0)
    norm_gain = jnp.clip(1.0 + 0.18 * jax.random.normal(arg_keys[6], (D,), jnp.float32), 0.1, 1.9)
    weight_in = centred(arg_keys[7], (EXPERTS, D, FF), D ** -0.5, 0.21875, ((0, 128),))
    weight_out = centred(arg_keys[8], (EXPERTS, FF, D), FF ** -0.5, 0.109375, ((0, 128),))
    old_place = jax.random.permutation(arg_keys[9], EXPERTS).astype(jnp.int32)
    partner = draw_partner(jax.random.fold_in(arg_keys[11], 71), 0)
    return {"group_one": group_one, "routes_one": routes_one, "gates_one": gates_one, "group_two": group_two, "routes_two": routes_two, "gates_two": gates_two, "norm_gain": norm_gain, "weight_in": weight_in, "weight_out": weight_out, "old_place": old_place, "partner": partner}


epsilon = 1e-06

def expert_table(routes):
    expert_ids = routes[:, 0].astype(jnp.int32)
    ordering = jnp.argsort(expert_ids, stable=True).astype(jnp.int32)
    sorted_ids = expert_ids[ordering]
    counts = jnp.zeros((EXPERTS,), jnp.int32).at[expert_ids].add(1)
    starts = jnp.cumsum(counts).astype(jnp.int32) - counts
    placed = jnp.arange(TOKENS, dtype=jnp.int32) - starts[sorted_ids]
    row_table = jnp.full((EXPERTS, EXPERT_ROWS), TOKENS, jnp.int32)
    return row_table.at[sorted_ids, placed].set(ordering)

def switch_layer(tokens_in, routes, gate_probs, norm_gain, weight_in, weight_out, holder):
    values = tokens_in.astype(jnp.float32)
    scaling = lax.rsqrt(lax.optimization_barrier(jnp.mean(values * values, axis=1, keepdims=True)) + epsilon)
    normed = (values * scaling * norm_gain.astype(jnp.float32)).astype(jnp.bfloat16)
    padded = jnp.concatenate([normed, jnp.zeros((1, D), jnp.bfloat16)], axis=0)
    row_table = expert_table(routes)

    def one_expert(members):
        entries, holder_slot = members
        inputs = padded[entries]
        hidden = jnp.maximum(jnp.dot(inputs, weight_in[holder_slot], preferred_element_type=jnp.float32), 0.0).astype(jnp.bfloat16)
        return jnp.dot(hidden, weight_out[holder_slot], preferred_element_type=jnp.float32).astype(jnp.bfloat16)
    outputs = lax.map(one_expert, (row_table, holder))
    gathered = jnp.zeros((TOKENS + 1, D), jnp.bfloat16).at[row_table].set(outputs)[:TOKENS]
    mixed = values + gate_probs.astype(jnp.float32)[:, None] * gathered.astype(jnp.float32)
    return mixed.astype(jnp.bfloat16)

def reference(group_one, routes_one, gates_one, group_two, routes_two, gates_two, norm_gain, weight_in, weight_out, old_place, partner):
    holder = jnp.argsort(old_place).astype(jnp.int32)
    first_out = switch_layer(group_one, routes_one, gates_one, norm_gain, weight_in, weight_out, holder)
    second = switch_layer(group_two, routes_two, gates_two, norm_gain, weight_in, weight_out, holder)
    new_in = jnp.take(weight_in, partner, axis=0)
    new_out = jnp.take(weight_out, partner, axis=0)
    return (first_out, second, new_in, new_out)
```

```python
import functools

import jax
import jax.numpy as jnp
from jax import lax
from jax.experimental import pallas as pl
from jax.experimental.pallas import tpu as pltpu
from jax.sharding import PartitionSpec as P

AXES = ("gx", "gy")
EPS = 1e-06
CAP = 6
N = 128
HALF = 2304
CHUNK = 72
TOK = 9
C1, C2, C3 = 21, 20, 21
NPART = 41
MA2 = 10
MB2 = C2 - MA2

HBM = pl.BlockSpec(memory_space=pltpu.MemorySpace.HBM)
SMEM = pl.BlockSpec(memory_space=pltpu.SMEM)
VMEM = pl.BlockSpec(memory_space=pltpu.VMEM)
BF = jnp.bfloat16


def tiles_of(w, rows, cols):
    return w.reshape(rows // 8, 8, cols // 128, 128).transpose(0, 2, 1, 3).reshape(HALF, 8, 128)


def array_of(t, rows, cols):
    return t.reshape(rows // 8, cols // 128, 8, 128).transpose(0, 2, 1, 3).reshape(1, rows, cols)


def copies(partner, visit):
    def step(j, counts):
        movers, stayers = counts
        p = partner[j]
        moving = p != j
        visit(j, moving, jnp.where(moving, movers, stayers), p)
        one = moving.astype(jnp.int32)
        return (movers + one, stayers + 1 - one)

    lax.fori_loop(0, N, step, (jnp.int32(0), jnp.int32(0)))


def own_piece(w_in, w_out, rank, offset, size, act):
    @pl.when(rank < 32)
    def _():
        act(w_in.at[pl.ds(rank * CHUNK + offset, size)])

    @pl.when(rank >= 32)
    def _():
        act(w_out.at[pl.ds((rank - 32) * CHUNK + offset, size)])


def go(src, dst, sem, wait):
    copy = pltpu.make_async_copy(src, dst, sem)
    if wait:
        copy.wait()
    else:
        copy.start()


def first_kernel(
    me, partner, w_in, w_out, one, two, routes_one, routes_two, gain, place,
    buf1, pos, tok, sem, tsem,
):
    my = me[0]
    i_move = partner[my] != my

    def sends(wait):
        def visit(j, moving, rank, p):
            offset = jnp.where(moving, NPART, 0)
            own_piece(
                w_in, w_out, rank, offset, C1,
                lambda src: go(src, buf1.at[j, pl.ds(0, C1)], sem, wait),
            )

        @pl.when(i_move)
        def _():
            copies(partner, visit)

    sends(False)
    rows = one.shape[0]
    width = one.shape[1]
    total = 2 * rows
    slots = place[...]
    lower = (
        lax.broadcasted_iota(jnp.int32, (rows, rows), 1)
        < lax.broadcasted_iota(jnp.int32, (rows, rows), 0)
    ).astype(jnp.float32).astype(BF)
    lane = lax.broadcasted_iota(jnp.int32, (rows, N), 1)
    normed, target, place_in = [], [], []
    for b, (group, routes) in enumerate(((one, routes_one), (two, routes_two))):
        values = group[...].astype(jnp.float32)
        scaling = lax.rsqrt(jnp.mean(values * values, axis=1, keepdims=True) + EPS)
        normed.append((values * scaling * gain[...]).astype(BF))
        member = routes[...] == slots
        flag = member.astype(jnp.float32)
        before = jnp.dot(lower, flag.astype(BF), preferred_element_type=jnp.float32)
        target.append(jnp.sum(jnp.where(member, lane, 0), axis=1, keepdims=True))
        place_in.append(
            jnp.sum(flag * before, axis=1, keepdims=True).astype(jnp.int32) + b * CAP
        )
    normed = jnp.concatenate(normed, axis=0)
    target = jnp.concatenate(target, axis=0)
    place_in = jnp.concatenate(place_in, axis=0)
    early = jnp.where(place_in < 8, target * 8 + place_in, -1)
    late = jnp.where(place_in < 8, -1, target * 8 + place_in - 8)
    pos[:, 0:1] = early
    pos[:, 1:2] = late
    eye = lax.broadcasted_iota(jnp.int32, (total, total), 0) == lax.broadcasted_iota(
        jnp.int32, (total, total), 1
    )
    early_row = jnp.sum(jnp.where(eye, early, 0), axis=0, keepdims=True)
    late_row = jnp.sum(jnp.where(eye, late, 0), axis=0, keepdims=True)
    row = lax.broadcasted_iota(jnp.int32, (N * 8, total), 0)
    pick = (row == early_row).astype(jnp.float32).astype(BF)
    top = jnp.dot(pick, normed, preferred_element_type=jnp.float32)
    fours = row - (row & 4)
    pick = (fours == late_row).astype(jnp.float32).astype(BF)
    rest = jnp.dot(pick, normed, preferred_element_type=jnp.float32)
    upper = lax.broadcasted_iota(jnp.int32, (N, 8, 128), 1) < 4
    cut = lambda x, c: x[:, c * 128 : (c + 1) * 128].reshape(N, 8, 128)
    for c in range(width // 128):
        tok[:, c] = cut(top, c).astype(BF)
    for c in range(width // 256):
        tok[:, width // 128 + c] = jnp.where(upper, cut(rest, 2 * c), cut(rest, 2 * c + 1)).astype(BF)
    go(tok, buf1.at[:, pl.ds(C1, TOK)], tsem, False)
    go(tok, buf1.at[:, pl.ds(C1, TOK)], tsem, True)
    sends(True)


def second_own_kernel(me, partner, w_in, w_out, buf2, sem):
    my = me[0]

    def sends(wait):
        def visit(j, moving, rank, p):
            @pl.when(moving)
            def _():
                own_piece(
                    w_in, w_out, rank, NPART + C1, MA2,
                    lambda src: go(src, buf2.at[j, pl.ds(0, MA2)], sem, wait),
                )

            @pl.when(jnp.logical_not(moving))
            def _():
                own_piece(
                    w_in, w_out, rank, C1, C2,
                    lambda src: go(src, buf2.at[j, pl.ds(0, C2)], sem, wait),
                )

        @pl.when(partner[my] != my)
        def _():
            copies(partner, visit)

    sends(False)
    sends(True)


def forward_kernel(of_mover, of_stayer, extra, me, partner, recv, *refs):
    if extra:
        tok, _, buf, sem, tsem = refs
        go(tok, buf.at[:, pl.ds(C3, TOK)], tsem, False)
    else:
        *_, buf, sem = refs
    my = me[0]
    i_move = partner[my] != my

    def sends(wait):
        for mine, (lo, to, size) in ((True, of_mover), (False, of_stayer)):
            def visit(j, moving, rank, p):
                @pl.when(moving)
                def _():
                    go(recv.at[p, pl.ds(lo, size)], buf.at[j, pl.ds(to, size)], sem, wait)

            @pl.when(i_move == mine)
            def _():
                copies(partner, visit)

    sends(False)
    sends(True)
    if extra:
        go(tok, buf.at[:, pl.ds(C3, TOK)], tsem, True)


def settle(partner, recv, new_in, new_out, sem, wait, of_mover, of_stayer):
    def visit(j, moving, rank, p):
        for kind, (lo, to, size) in ((True, of_mover), (False, of_stayer)):
            @pl.when(moving == kind)
            def _():
                own_piece(
                    new_in, new_out, rank, to, size,
                    lambda dst: go(recv.at[j, pl.ds(lo, size)], dst, sem, wait),
                )

    copies(partner, visit)


def third_settle_kernel(me, partner, w_in, w_out, recv2, new_in, new_out, sem):
    my = me[0]
    i_move = partner[my] != my

    def sends(wait):
        @pl.when(i_move)
        def _():
            settle(
                partner, recv2, new_in, new_out, sem, wait,
                (MA2, NPART, MB2), (0, 0, C2),
            )

        @pl.when(jnp.logical_not(i_move))
        def _():
            go(w_in, new_in, sem, wait)
            go(w_out, new_out, sem, wait)

    sends(False)
    sends(True)


def last_kernel(
    me, partner, recv3, pos, one, two, gate_one, gate_two, in_, out_,
    res_one, res_two, new_in, new_out, tok, sem, tsem,
):
    my = me[0]
    i_move = partner[my] != my

    go(recv3.at[:, pl.ds(C3, TOK)], tok, tsem, False)

    def sends(wait):
        @pl.when(i_move)
        def _():
            settle(
                partner, recv3, new_in, new_out, sem, wait,
                (0, NPART + MB2, C3), (0, C2, C3),
            )

    sends(False)
    go(recv3.at[:, pl.ds(C3, TOK)], tok, tsem, True)
    rows = one.shape[0]
    width = one.shape[1]
    total = 2 * rows
    early = pos[:, 0:1]
    late = pos[:, 1:2]
    lane = lax.broadcasted_iota(jnp.int32, (total, N * 8), 1)
    hot = lambda where: (lane == where).astype(jnp.float32).astype(BF)
    flat = lambda c: tok[:, c].astype(jnp.float32).reshape(N * 8, 128).astype(BF)
    full = jnp.concatenate([flat(c) for c in range(width // 128)], axis=1)
    tail = jnp.concatenate([flat(width // 128 + c) for c in range(width // 256)], axis=1)
    top = jnp.dot(hot(early), full, preferred_element_type=jnp.float32)
    even = jnp.dot(hot(late), tail, preferred_element_type=jnp.float32)
    odd = jnp.dot(
        hot(jnp.where(late < 0, -1, late + 4)), tail, preferred_element_type=jnp.float32
    )
    for b, (group, gate, res) in enumerate(
        ((one, gate_one, res_one), (two, gate_two, res_two))
    ):
        r = slice(b * rows, (b + 1) * rows)
        for c in range(width // 128):
            s = slice(c * 128, (c + 1) * 128)
            h = slice(c // 2 * 128, (c // 2 + 1) * 128)
            answer = top[r, s] + (odd if c % 2 else even)[r, h]
            res[:, s] = (group[:, s].astype(jnp.float32) + gate[...] * answer).astype(BF)
    sends(True)


def shape(*dims, dtype=BF):
    return jax.ShapeDtypeStruct(dims, dtype)


def exchange(x):
    return lax.all_to_all(x, AXES, split_axis=0, concat_axis=0, tiled=True)


DMA = pltpu.SemaphoreType.DMA(())


def local(
    group_one, routes_one, gates_one, group_two, routes_two, gates_two,
    norm_gain, weight_in, weight_out, old_place, partner,
):
    rows, width = group_one.shape
    ff = weight_in.shape[2]
    me = lax.axis_index(AXES).astype(jnp.int32).reshape(1)
    w_in = tiles_of(weight_in, width, ff)
    w_out = tiles_of(weight_out, ff, width)
    buf1, pos = pl.pallas_call(
        first_kernel,
        out_shape=(shape(N, C1 + TOK, 8, 128), shape(2 * rows, 2, dtype=jnp.int32)),
        in_specs=[SMEM, SMEM, HBM, HBM] + [VMEM] * 6,
        out_specs=(HBM, VMEM),
        scratch_shapes=[pltpu.VMEM((N, TOK, 8, 128), BF), DMA, DMA],
        name="first",
    )(
        me, partner, w_in, w_out, group_one, group_two, routes_one, routes_two,
        norm_gain.reshape(1, width), old_place.reshape(1, N),
    )
    recv1 = exchange(buf1)
    buf2 = pl.pallas_call(
        second_own_kernel,
        out_shape=shape(N, C2, 8, 128),
        in_specs=[SMEM, SMEM, HBM, HBM],
        out_specs=HBM,
        scratch_shapes=[DMA],
        name="second_own",
    )(me, partner, w_in, w_out)
    buf2 = pl.pallas_call(
        functools.partial(forward_kernel, (0, MA2, MB2), (0, 0, C2), False),
        out_shape=shape(N, C2, 8, 128),
        in_specs=[SMEM, SMEM, HBM, HBM],
        out_specs=HBM,
        scratch_shapes=[DMA],
        input_output_aliases={3: 0},
        name="second_forward",
    )(me, partner, recv1, buf2)
    recv2 = exchange(buf2)
    arrived = recv1[:, C1:]
    cols = width // 128
    top = arrived[:, :cols].transpose(0, 2, 1, 3).reshape(N * 8, width)
    rest = arrived[:, cols:].reshape(N, cols // 2, 2, 4, 128)
    rest = rest.transpose(0, 3, 1, 2, 4).reshape(N * 4, width)
    inputs = jnp.concatenate([top, rest], axis=0)
    hidden = jnp.maximum(
        jnp.dot(inputs, weight_in[0], preferred_element_type=jnp.float32), 0.0
    ).astype(BF)
    result = jnp.dot(hidden, weight_out[0], preferred_element_type=jnp.float32).astype(BF)
    top = result[: N * 8].reshape(N, 8, cols, 128).transpose(0, 2, 1, 3)
    rest = result[N * 8 :].reshape(N, 4, cols // 2, 2, 128)
    rest = rest.transpose(0, 2, 3, 1, 4).reshape(N, cols // 2, 8, 128)
    answers = jnp.concatenate([top, rest], axis=1)
    buf3 = pl.pallas_call(
        functools.partial(
            forward_kernel, (MB2, 0, C1 - MB2), (C2, 0, C1 - C2), False
        ),
        out_shape=shape(N, C3 + TOK, 8, 128),
        in_specs=[SMEM, SMEM, HBM],
        out_specs=HBM,
        scratch_shapes=[DMA],
        name="third_held",
    )(me, partner, recv1)
    buf3 = pl.pallas_call(
        functools.partial(
            forward_kernel, (0, C1 - MB2, MA2), (0, C1 - C2, C2), True
        ),
        out_shape=shape(N, C3 + TOK, 8, 128),
        in_specs=[SMEM, SMEM, HBM, pl.BlockSpec(memory_space=pl.ANY), HBM],
        out_specs=HBM,
        scratch_shapes=[DMA, DMA],
        input_output_aliases={4: 0},
        name="third_forward",
    )(me, partner, recv2, answers, buf3)
    recv3 = exchange(buf3)
    new_in, new_out = pl.pallas_call(
        third_settle_kernel,
        out_shape=(shape(HALF, 8, 128), shape(HALF, 8, 128)),
        in_specs=[SMEM, SMEM, HBM, HBM, HBM],
        out_specs=(HBM, HBM),
        scratch_shapes=[DMA],
        name="settle",
    )(me, partner, w_in, w_out, recv2)
    res_one, res_two, new_in, new_out = pl.pallas_call(
        last_kernel,
        out_shape=(
            shape(rows, width), shape(rows, width), shape(HALF, 8, 128), shape(HALF, 8, 128),
        ),
        in_specs=[SMEM, SMEM, HBM] + [VMEM] * 5 + [HBM, HBM],
        out_specs=(VMEM, VMEM, HBM, HBM),
        scratch_shapes=[pltpu.VMEM((N, TOK, 8, 128), BF), DMA, DMA],
        input_output_aliases={8: 2, 9: 3},
        name="last",
    )(
        me, partner, recv3, pos, group_one, group_two,
        gates_one.reshape(rows, 1), gates_two.reshape(rows, 1), new_in, new_out,
    )
    return (res_one, res_two, array_of(new_in, width, ff), array_of(new_out, ff, width))


def solution(mesh):
    split = P(AXES, None)
    flat = P(AXES)
    deep = P(AXES, None, None)
    return jax.shard_map(
        local,
        mesh=mesh,
        in_specs=(split, split, flat, split, split, flat, P(), deep, deep, P(), P()),
        out_specs=(split, split, deep, deep),
        check_vma=False,
    )
```

```python
import functools

import jax
import jax.numpy as jnp
from jax import lax
from jax.experimental import pallas as pl
from jax.experimental.pallas import tpu as pltpu
from jax.sharding import PartitionSpec as P

AXES = ("gx", "gy")
EPS = 1e-06
CAP = 6
N = 128
HALF = 2304
CHUNK = 72
TOK = 9
C1, C2, C3 = 21, 20, 21
NPART = 41
MA2 = 10
MB2 = C2 - MA2
GROUPS = 8
SIZE = N // GROUPS

HBM = pl.BlockSpec(memory_space=pltpu.MemorySpace.HBM)
SMEM = pl.BlockSpec(memory_space=pltpu.SMEM)
VMEM = pl.BlockSpec(memory_space=pltpu.VMEM)
BF = jnp.bfloat16


def tiles_of(w, rows, cols):
    return w.reshape(rows // 8, 8, cols // 128, 128).transpose(0, 2, 1, 3).reshape(HALF, 8, 128)


def array_of(t, rows, cols):
    return t.reshape(rows // 8, cols // 128, 8, 128).transpose(0, 2, 1, 3).reshape(1, rows, cols)


def copies(partner, visit, after=None):
    def step(j, counts):
        movers, stayers = counts
        p = partner[j]
        moving = p != j
        visit(j, moving, jnp.where(moving, movers, stayers), p)
        one = moving.astype(jnp.int32)
        return (movers + one, stayers + 1 - one)

    def group(g, counts):
        counts = lax.fori_loop(g * SIZE, (g + 1) * SIZE, step, counts)
        if after is not None:
            after(g)
        return counts

    lax.fori_loop(0, GROUPS, group, (jnp.int32(0), jnp.int32(0)))


def own_piece(w_in, w_out, rank, offset, size, act):
    @pl.when(rank < 32)
    def _():
        act(w_in.at[pl.ds(rank * CHUNK + offset, size)])

    @pl.when(rank >= 32)
    def _():
        act(w_out.at[pl.ds((rank - 32) * CHUNK + offset, size)])


def go(src, dst, sem, wait):
    copy = pltpu.make_async_copy(src, dst, sem)
    if wait:
        copy.wait()
    else:
        copy.start()


def nothing(j, moving, rank, p):
    pass


def column(row):
    n = row.shape[1]
    eye = lax.broadcasted_iota(jnp.int32, (n, n), 0) == lax.broadcasted_iota(jnp.int32, (n, n), 1)
    return jnp.sum(jnp.where(eye, row, 0), axis=1, keepdims=True)


def first_kernel(
    me, partner, w_in, w_out, one, two, routes_one, routes_two, gain, place,
    buf1, pos, stage, sem, osem,
):
    my = me[0]
    i_move = partner[my] != my

    def visit(wait, j, moving, rank, p):
        offset = jnp.where(moving, NPART, 0)
        own_piece(
            w_in, w_out, rank, offset, C1,
            lambda src: go(src, stage.at[j, pl.ds(0, C1)], sem.at[j // SIZE], wait),
        )

    @pl.when(i_move)
    def _():
        copies(partner, functools.partial(visit, False))

    rows = one.shape[0]
    width = one.shape[1]
    cols = width // 128
    total = 2 * rows
    slots = place[...]
    lower = (
        lax.broadcasted_iota(jnp.int32, (rows, rows), 1)
        < lax.broadcasted_iota(jnp.int32, (rows, rows), 0)
    ).astype(jnp.float32).astype(BF)
    lane = lax.broadcasted_iota(jnp.int32, (rows, N), 1)
    normed, target, place_in = [], [], []
    for b, (group, routes) in enumerate(((one, routes_one), (two, routes_two))):
        values = group[...].astype(jnp.float32)
        scaling = lax.rsqrt(jnp.mean(values * values, axis=1, keepdims=True) + EPS)
        normed.append((values * scaling * gain[...]).astype(BF))
        member = column(routes[...]) == slots
        flag = member.astype(jnp.float32)
        before = jnp.dot(lower, flag.astype(BF), preferred_element_type=jnp.float32)
        target.append(jnp.sum(jnp.where(member, lane, 0), axis=1, keepdims=True))
        place_in.append(
            jnp.sum(flag * before, axis=1, keepdims=True).astype(jnp.int32) + b * CAP
        )
    normed = jnp.concatenate(normed, axis=0)
    target = jnp.concatenate(target, axis=0)
    place_in = jnp.concatenate(place_in, axis=0)
    early = jnp.where(place_in < 8, target * 8 + place_in, -1)
    late = jnp.where(place_in < 8, -1, target * 8 + place_in - 8)
    pos[:, 0:1] = early
    pos[:, 1:2] = late

    def out(wait, lo, size, g):
        part = pl.ds(g * SIZE, SIZE)
        go(stage.at[part, pl.ds(lo, size)], buf1.at[part, pl.ds(lo, size)], osem, wait)

    @pl.when(i_move)
    def _():
        copies(partner, functools.partial(visit, True), functools.partial(out, False, 0, C1))

    eye = lax.broadcasted_iota(jnp.int32, (total, total), 0) == lax.broadcasted_iota(
        jnp.int32, (total, total), 1
    )
    early_row = jnp.sum(jnp.where(eye, early, 0), axis=0, keepdims=True)
    late_row = jnp.sum(jnp.where(eye, late, 0), axis=0, keepdims=True)
    row = lax.broadcasted_iota(jnp.int32, (N * 8, total), 0)
    pick = (row == early_row).astype(jnp.float32).astype(BF)
    top = jnp.dot(pick, normed, preferred_element_type=jnp.float32)
    fours = row - (row & 4)
    pick = (fours == late_row).astype(jnp.float32).astype(BF)
    rest = jnp.dot(pick, normed, preferred_element_type=jnp.float32)
    upper = lax.broadcasted_iota(jnp.int32, (N, 8, 128), 1) < 4
    cut = lambda x, c: x[:, c * 128 : (c + 1) * 128].reshape(N, 8, 128)
    for c in range(cols):
        stage[:, C1 + c] = cut(top, c).astype(BF)
    for c in range(cols // 2):
        stage[:, C1 + cols + c] = jnp.where(upper, cut(rest, 2 * c), cut(rest, 2 * c + 1)).astype(BF)
    for g in range(GROUPS):
        out(False, C1, TOK, g)
    for g in range(GROUPS):
        out(True, C1, TOK, g)

    @pl.when(i_move)
    def _():
        copies(partner, nothing, functools.partial(out, True, 0, C1))


def second_kernel(me, partner, w_in, w_out, recv1, buf2, stage, sem, osem):
    my = me[0]
    i_move = partner[my] != my

    def from_mover(wait, j, moving, rank, p):
        at = sem.at[j // SIZE]

        @pl.when(moving)
        def _():
            own_piece(
                w_in, w_out, rank, NPART + C1, MA2,
                lambda src: go(src, stage.at[j, pl.ds(0, MA2)], at, wait),
            )
            go(recv1.at[p, pl.ds(0, MB2)], stage.at[j, pl.ds(MA2, MB2)], at, wait)

        @pl.when(jnp.logical_not(moving))
        def _():
            own_piece(
                w_in, w_out, rank, C1, C2,
                lambda src: go(src, stage.at[j, pl.ds(0, C2)], at, wait),
            )

    def from_stayer(wait, j, moving, rank, p):
        @pl.when(moving)
        def _():
            go(recv1.at[p, pl.ds(0, C2)], stage.at[j, pl.ds(0, C2)], sem.at[j // SIZE], wait)

    def out(wait, g):
        part = pl.ds(g * SIZE, SIZE)
        go(stage.at[part], buf2.at[part], osem, wait)

    for mine, visit in ((True, from_mover), (False, from_stayer)):
        @pl.when(i_move == mine)
        def _():
            copies(partner, functools.partial(visit, False))
            copies(partner, functools.partial(visit, True), functools.partial(out, False))
            copies(partner, nothing, functools.partial(out, True))


def third_kernel(me, partner, recv1, recv2, answers, buf3, stage, sem, osem):
    my = me[0]
    i_move = partner[my] != my

    def visit(early, late, wait, j, moving, rank, p):
        at = sem.at[j // SIZE]

        @pl.when(moving)
        def _():
            go(recv1.at[p, pl.ds(early, C1 - late)], stage.at[j, pl.ds(0, C1 - late)], at, wait)
            go(recv2.at[p, pl.ds(0, late)], stage.at[j, pl.ds(C1 - late, late)], at, wait)

    def token(wait, g):
        part = pl.ds(g * SIZE, SIZE)
        go(answers.at[part], stage.at[part, pl.ds(C3, TOK)], sem.at[g], wait)

    def out(wait, g):
        part = pl.ds(g * SIZE, SIZE)
        if not wait:
            token(True, g)
        go(stage.at[part], buf3.at[part], osem, wait)

    for mine, early, late in ((True, MB2, MA2), (False, C2, C2)):
        step = functools.partial(visit, early, late)

        @pl.when(i_move == mine)
        def _():
            copies(partner, functools.partial(step, False), functools.partial(token, False))
            copies(partner, functools.partial(step, True), functools.partial(out, False))
            copies(partner, nothing, functools.partial(out, True))


def settle_kernel(me, partner, w_in, w_out, recv2, new_in, new_out, stage, sem, osem):
    my = me[0]
    i_move = partner[my] != my

    def load(wait, g):
        part = pl.ds(g * SIZE * C2, SIZE * C2)
        go(recv2.at[part], stage.at[part], sem.at[g], wait)

    def visit(wait, j, moving, rank, p):
        if not wait:
            @pl.when(j % SIZE == 0)
            def _():
                load(True, j // SIZE)

        @pl.when(moving)
        def _():
            own_piece(
                new_in, new_out, rank, NPART, MB2,
                lambda dst: go(stage.at[pl.ds(j * C2 + MA2, MB2)], dst, osem, wait),
            )

        @pl.when(jnp.logical_not(moving))
        def _():
            own_piece(
                new_in, new_out, rank, 0, C2,
                lambda dst: go(stage.at[pl.ds(j * C2, C2)], dst, osem, wait),
            )

    @pl.when(i_move)
    def _():
        copies(partner, nothing, functools.partial(load, False))
        copies(partner, functools.partial(visit, False))
        copies(partner, functools.partial(visit, True))

    @pl.when(jnp.logical_not(i_move))
    def _():
        size = HALF // GROUPS
        pieces = [
            (src.at[pl.ds(g * size, size)], stage.at[pl.ds(h * HALF + g * size, size)],
             dst.at[pl.ds(g * size, size)], g)
            for h, (src, dst) in enumerate(((w_in, new_in), (w_out, new_out)))
            for g in range(GROUPS)
        ]
        for h in range(2):
            half = pieces[h * GROUPS : (h + 1) * GROUPS]
            for src, mid, dst, g in half:
                go(src, mid, sem.at[g], False)
            for src, mid, dst, g in half:
                go(src, mid, sem.at[g], True)
                go(mid, dst, osem, False)
        for src, mid, dst, g in pieces:
            go(mid, dst, osem, True)


def last_kernel(
    me, partner, recv3, pos, one, two, gate_one, gate_two, in_, out_,
    res_one, res_two, new_in, new_out, stage, sem, osem,
):
    my = me[0]
    i_move = partner[my] != my

    def load(wait, g):
        part = pl.ds(g * SIZE, SIZE)
        go(recv3.at[part], stage.at[part], sem.at[g], wait)

    def visit(wait, j, moving, rank, p):
        offset = jnp.where(moving, NPART + MB2, C2)
        own_piece(
            new_in, new_out, rank, offset, C3,
            lambda dst: go(stage.at[j, pl.ds(0, C3)], dst, osem, wait),
        )

    for g in range(GROUPS):
        load(False, g)
    for g in range(GROUPS):
        load(True, g)

    @pl.when(i_move)
    def _():
        copies(partner, functools.partial(visit, False))

    rows = one.shape[0]
    width = one.shape[1]
    cols = width // 128
    total = 2 * rows
    early = pos[:, 0:1]
    late = pos[:, 1:2]
    lane = lax.broadcasted_iota(jnp.int32, (total, N * 8), 1)
    hot = lambda where: (lane == where).astype(jnp.float32).astype(BF)
    flat = lambda c: stage[:, C3 + c].astype(jnp.float32).reshape(N * 8, 128).astype(BF)
    full = jnp.concatenate([flat(c) for c in range(cols)], axis=1)
    tail = jnp.concatenate([flat(cols + c) for c in range(cols // 2)], axis=1)
    top = jnp.dot(hot(early), full, preferred_element_type=jnp.float32)
    even = jnp.dot(hot(late), tail, preferred_element_type=jnp.float32)
    odd = jnp.dot(
        hot(jnp.where(late < 0, -1, late + 4)), tail, preferred_element_type=jnp.float32
    )
    for b, (group, gate, res) in enumerate(
        ((one, gate_one, res_one), (two, gate_two, res_two))
    ):
        r = slice(b * rows, (b + 1) * rows)
        for c in range(cols):
            s = slice(c * 128, (c + 1) * 128)
            h = slice(c // 2 * 128, (c // 2 + 1) * 128)
            answer = top[r, s] + (odd if c % 2 else even)[r, h]
            res[:, s] = (group[:, s].astype(jnp.float32) + gate[...] * answer).astype(BF)

    @pl.when(i_move)
    def _():
        copies(partner, functools.partial(visit, True))


def shape(*dims, dtype=BF):
    return jax.ShapeDtypeStruct(dims, dtype)


def exchange(x):
    return lax.all_to_all(x, AXES, split_axis=0, concat_axis=0, tiled=True)


DMA = pltpu.SemaphoreType.DMA(())
SEMS = pltpu.SemaphoreType.DMA((GROUPS,))


def local(
    group_one, routes_one, gates_one, group_two, routes_two, gates_two,
    norm_gain, weight_in, weight_out, old_place, partner,
):
    rows, width = group_one.shape
    ff = weight_in.shape[2]
    me = lax.axis_index(AXES).astype(jnp.int32).reshape(1)
    w_in = tiles_of(weight_in, width, ff)
    w_out = tiles_of(weight_out, ff, width)
    buf1, pos = pl.pallas_call(
        first_kernel,
        out_shape=(shape(N, C1 + TOK, 8, 128), shape(2 * rows, 2, dtype=jnp.int32)),
        in_specs=[SMEM, SMEM, HBM, HBM] + [VMEM] * 6,
        out_specs=(HBM, VMEM),
        scratch_shapes=[pltpu.VMEM((N, C1 + TOK, 8, 128), BF), SEMS, DMA],
        name="first",
    )(
        me, partner, w_in, w_out, group_one, group_two,
        routes_one.reshape(1, rows), routes_two.reshape(1, rows),
        norm_gain.reshape(1, width), old_place.reshape(1, N),
    )
    recv1 = exchange(buf1)
    buf2 = pl.pallas_call(
        second_kernel,
        out_shape=shape(N, C2, 8, 128),
        in_specs=[SMEM, SMEM, HBM, HBM, HBM],
        out_specs=HBM,
        scratch_shapes=[pltpu.VMEM((N, C2, 8, 128), BF), SEMS, DMA],
        name="second",
    )(me, partner, w_in, w_out, recv1)
    recv2 = exchange(buf2)
    arrived = recv1[:, C1:]
    cols = width // 128
    top = arrived[:, :cols].transpose(0, 2, 1, 3).reshape(N * 8, width)
    rest = arrived[:, cols:].reshape(N, cols // 2, 2, 4, 128)
    rest = rest.transpose(0, 3, 1, 2, 4).reshape(N * 4, width)
    inputs = jnp.concatenate([top, rest], axis=0)
    hidden = jnp.maximum(
        jnp.dot(inputs, weight_in[0], preferred_element_type=jnp.float32), 0.0
    ).astype(BF)
    result = jnp.dot(hidden, weight_out[0], preferred_element_type=jnp.float32).astype(BF)
    top = result[: N * 8].reshape(N, 8, cols, 128).transpose(0, 2, 1, 3)
    rest = result[N * 8 :].reshape(N, 4, cols // 2, 2, 128)
    rest = rest.transpose(0, 2, 3, 1, 4).reshape(N, cols // 2, 8, 128)
    answers = jnp.concatenate([top, rest], axis=1)
    buf3 = pl.pallas_call(
        third_kernel,
        out_shape=shape(N, C3 + TOK, 8, 128),
        in_specs=[SMEM, SMEM, HBM, HBM, pl.BlockSpec(memory_space=pl.ANY)],
        out_specs=HBM,
        scratch_shapes=[pltpu.VMEM((N, C3 + TOK, 8, 128), BF), SEMS, DMA],
        name="third",
    )(me, partner, recv1, recv2, answers)
    recv3 = exchange(buf3)
    new_in, new_out = pl.pallas_call(
        settle_kernel,
        out_shape=(shape(HALF, 8, 128), shape(HALF, 8, 128)),
        in_specs=[SMEM, SMEM, HBM, HBM, HBM],
        out_specs=(HBM, HBM),
        scratch_shapes=[pltpu.VMEM((2 * HALF, 8, 128), BF), SEMS, DMA],
        name="settle",
    )(me, partner, w_in, w_out, recv2.reshape(N * C2, 8, 128))
    res_one, res_two, new_in, new_out = pl.pallas_call(
        last_kernel,
        out_shape=(
            shape(rows, width), shape(rows, width), shape(HALF, 8, 128), shape(HALF, 8, 128),
        ),
        in_specs=[SMEM, SMEM, HBM] + [VMEM] * 5 + [HBM, HBM],
        out_specs=(VMEM, VMEM, HBM, HBM),
        scratch_shapes=[pltpu.VMEM((N, C3 + TOK, 8, 128), BF), SEMS, DMA],
        input_output_aliases={8: 2, 9: 3},
        name="last",
    )(
        me, partner, recv3, pos, group_one, group_two,
        gates_one.reshape(rows, 1), gates_two.reshape(rows, 1), new_in, new_out,
    )
    return (res_one, res_two, array_of(new_in, width, ff), array_of(new_out, ff, width))


def solution(mesh):
    split = P(AXES, None)
    flat = P(AXES)
    deep = P(AXES, None, None)
    return jax.shard_map(
        local,
        mesh=mesh,
        in_specs=(split, split, flat, split, split, flat, P(), deep, deep, P(), P()),
        out_specs=(split, split, deep, deep),
        check_vma=False,
    )
```

```python
import functools

import jax
import jax.numpy as jnp
from jax import lax
from jax.experimental import pallas as pl
from jax.experimental.pallas import tpu as pltpu
from jax.sharding import PartitionSpec as P

AXES = ("gx", "gy")
EPS = 1e-06
CAP = 6
N = 128
HALF = 2304
CHUNK = 72
TOK = 9
C1, C2, C3 = 21, 20, 21
NPART = 41
MA2 = 10
MB2 = C2 - MA2
GROUPS = 8
SIZE = N // GROUPS
UNROLL = 4

HBM = pl.BlockSpec(memory_space=pltpu.MemorySpace.HBM)
SMEM = pl.BlockSpec(memory_space=pltpu.SMEM)
VMEM = pl.BlockSpec(memory_space=pltpu.VMEM)
BF = jnp.bfloat16


def tiles_of(w, rows, cols):
    return w.reshape(rows // 8, 8, cols // 128, 128).transpose(0, 2, 1, 3).reshape(HALF, 8, 128)


def array_of(t, rows, cols):
    return t.reshape(rows // 8, cols // 128, 8, 128).transpose(0, 2, 1, 3).reshape(1, rows, cols)


def copies(partner, visit, after=None):
    def step(j, counts):
        movers, stayers = counts
        p = partner[j]
        moving = p != j
        visit(j, moving, jnp.where(moving, movers, stayers), p)
        one = moving.astype(jnp.int32)
        return (movers + one, stayers + 1 - one)

    def group(g, counts):
        counts = lax.fori_loop(g * SIZE, (g + 1) * SIZE, step, counts)
        if after is not None:
            after(g)
        return counts

    lax.fori_loop(0, GROUPS, group, (jnp.int32(0), jnp.int32(0)))


def own_piece(w_in, w_out, rank, offset, size, act):
    @pl.when(rank < 32)
    def _():
        act(w_in.at[pl.ds(rank * CHUNK + offset, size)])

    @pl.when(rank >= 32)
    def _():
        act(w_out.at[pl.ds((rank - 32) * CHUNK + offset, size)])


def go(src, dst, sem, wait):
    copy = pltpu.make_async_copy(src, dst, sem)
    if wait:
        copy.wait()
    else:
        copy.start()


def nothing(j, moving, rank, p):
    pass


def column(row):
    n = row.shape[1]
    eye = lax.broadcasted_iota(jnp.int32, (n, n), 0) == lax.broadcasted_iota(jnp.int32, (n, n), 1)
    return jnp.sum(jnp.where(eye, row, 0), axis=1, keepdims=True)


def both_halves(step, w_in, w_out):
    half = N // 4
    lax.fori_loop(0, half, lambda k, c: (step(k, w_in, k * CHUNK), c)[1], 0, unroll=UNROLL)
    lax.fori_loop(
        0, half, lambda k, c: (step(k + half, w_out, k * CHUNK), c)[1], 0, unroll=UNROLL
    )


def each_mover(step):
    lax.fori_loop(0, N // 2, lambda k, c: (step(k), c)[1], 0, unroll=UNROLL)


def settled(ref, sem):
    pltpu.make_async_copy(ref, ref, sem).wait()


def group_of(g):
    return pl.ds(g * SIZE, SIZE)


def first_kernel(
    me, partner, w_in, w_out, one, two, routes_one, routes_two, gain, place,
    buf1, pos, order, stage, sem, osem,
):
    my = me[0]
    i_move = partner[my] != my

    def sort(j, counts):
        movers, stayers = counts
        moving = partner[j] != j
        order[jnp.where(moving, movers, stayers)] = j
        one = moving.astype(jnp.int32)
        return (movers + one, stayers + 1 - one)

    lax.fori_loop(0, N, sort, (jnp.int32(0), jnp.int32(N // 2)), unroll=UNROLL)

    @pl.when(i_move)
    def _():
        def step(k, w, tile):
            m = order[k]
            t = order[k + N // 2]
            go(w.at[pl.ds(tile, C1)], stage.at[t, pl.ds(0, C1)], sem.at[t // SIZE], False)
            go(w.at[pl.ds(tile + NPART, C1)], stage.at[m, pl.ds(0, C1)], sem.at[m // SIZE], False)

        both_halves(step, w_in, w_out)

    rows = one.shape[0]
    width = one.shape[1]
    cols = width // 128
    total = 2 * rows
    slots = place[...]
    lower = (
        lax.broadcasted_iota(jnp.int32, (rows, rows), 1)
        < lax.broadcasted_iota(jnp.int32, (rows, rows), 0)
    ).astype(jnp.float32).astype(BF)
    lane = lax.broadcasted_iota(jnp.int32, (rows, N), 1)
    scale = jnp.concatenate([gain[c : c + 1, :] for c in range(cols)], axis=1)
    normed, target, place_in = [], [], []
    for b, (group, routes) in enumerate(((one, routes_one), (two, routes_two))):
        values = group[...].astype(jnp.float32)
        scaling = lax.rsqrt(jnp.mean(values * values, axis=1, keepdims=True) + EPS)
        normed.append((values * scaling * scale).astype(BF))
        member = column(routes[...]) == slots
        flag = member.astype(jnp.float32)
        before = jnp.dot(lower, flag.astype(BF), preferred_element_type=jnp.float32)
        target.append(jnp.sum(jnp.where(member, lane, 0), axis=1, keepdims=True))
        place_in.append(
            jnp.sum(flag * before, axis=1, keepdims=True).astype(jnp.int32) + b * CAP
        )
    normed = jnp.concatenate(normed, axis=0)
    target = jnp.concatenate(target, axis=0)
    place_in = jnp.concatenate(place_in, axis=0)
    early = jnp.where(place_in < 8, target * 8 + place_in, -1)
    late = jnp.where(place_in < 8, -1, target * 8 + place_in - 8)
    pos[:, 0:1] = early
    pos[:, 1:2] = late

    def tiles(lo, size):
        go(stage.at[:, pl.ds(lo, size)], buf1.at[:, pl.ds(lo, size)], osem, False)

    def out(lo, size, g):
        part = group_of(g)
        go(stage.at[part, pl.ds(lo, size)], buf1.at[part, pl.ds(lo, size)], osem, False)

    @pl.when(i_move)
    def _():
        for g in range(GROUPS):
            settled(stage.at[group_of(g), pl.ds(0, C1)], sem.at[g])
            out(0, C1, g)

    eye = lax.broadcasted_iota(jnp.int32, (total, total), 0) == lax.broadcasted_iota(
        jnp.int32, (total, total), 1
    )
    early_row = jnp.sum(jnp.where(eye, early, 0), axis=0, keepdims=True)
    late_row = jnp.sum(jnp.where(eye, late, 0), axis=0, keepdims=True)
    row = lax.broadcasted_iota(jnp.int32, (N * 8, total), 0)
    fours = row - (row & 4)
    upper = lax.broadcasted_iota(jnp.int32, (N, 8, 128), 1) < 4
    cut = lambda x, c: x[:, c * 128 : (c + 1) * 128].reshape(N, 8, 128)
    pick = (fours == late_row).astype(jnp.float32).astype(BF)
    rest = jnp.dot(pick, normed, preferred_element_type=jnp.float32)
    for c in range(cols // 2):
        stage[:, C1 + cols + c] = jnp.where(upper, cut(rest, 2 * c), cut(rest, 2 * c + 1)).astype(BF)
    tiles(C1 + cols, cols // 2)
    pick = (row == early_row).astype(jnp.float32).astype(BF)
    top = jnp.dot(pick, normed, preferred_element_type=jnp.float32)
    for c in range(cols):
        stage[:, C1 + c] = cut(top, c).astype(BF)
    tiles(C1, cols)
    settled(stage.at[:, pl.ds(C1, TOK)], osem)

    @pl.when(i_move)
    def _():
        settled(stage.at[:, pl.ds(0, C1)], osem)


def second_kernel(me, partner, order, w_in, w_out, recv1, buf2, stage, sem, osem):
    my = me[0]
    i_move = partner[my] != my

    @pl.when(i_move)
    def _():
        def step(k, w, tile):
            m = order[k]
            t = order[k + N // 2]
            at = sem.at[m // SIZE]
            go(w.at[pl.ds(tile + C1, C2)], stage.at[t], sem.at[t // SIZE], False)
            go(w.at[pl.ds(tile + NPART + C1, MA2)], stage.at[m, pl.ds(0, MA2)], at, False)
            go(recv1.at[partner[m], pl.ds(0, MB2)], stage.at[m, pl.ds(MA2, MB2)], at, False)

        both_halves(step, w_in, w_out)
        for g in range(GROUPS):
            settled(stage.at[group_of(g)], sem.at[g])
            go(stage.at[group_of(g)], buf2.at[group_of(g)], osem, False)
        settled(stage, osem)

    @pl.when(jnp.logical_not(i_move))
    def _():
        forward(order, partner, stage, buf2, sem, osem, C2, ((recv1, 0, 0, C2),))


def forward(order, partner, stage, buf, sem, osem, tiles, pieces, between=None):
    groups = N // 2 // SIZE

    def load(k):
        m = order[k]
        p = partner[m]
        for array, lo, to, size in pieces:
            go(array.at[p, pl.ds(lo, size)], stage.at[k, pl.ds(to, size)], sem.at[k // SIZE], False)

    each_mover(load)
    if between is not None:
        between()
    for g in range(groups):
        settled(stage.at[group_of(g), pl.ds(0, tiles)], sem.at[g])

        def send(i, c):
            k = g * SIZE + i
            go(stage.at[k, pl.ds(0, tiles)], buf.at[order[k], pl.ds(0, tiles)], osem, False)
            return c

        lax.fori_loop(0, SIZE, send, 0, unroll=UNROLL)
    settled(stage.at[pl.ds(0, N // 2), pl.ds(0, tiles)], osem)


def third_kernel(
    me, partner, order, recv1, recv2, answers, buf3, stage, tok, sem, osem, tsem
):
    my = me[0]
    i_move = partner[my] != my
    go(answers, tok, tsem, False)

    def tokens():
        go(answers, tok, tsem, True)
        go(tok, buf3.at[:, pl.ds(C3, TOK)], tsem, False)

    for mine, early, late in ((True, MB2, MA2), (False, C2, C2)):
        held = C1 - late

        @pl.when(i_move == mine)
        def _():
            forward(
                order, partner, stage, buf3, sem, osem, C3,
                ((recv1, early, 0, held), (recv2, 0, held, late)),
                tokens,
            )

    go(tok, buf3.at[:, pl.ds(C3, TOK)], tsem, True)


def settle_kernel(me, partner, w_in, w_out, recv2, new_in, new_out, stage, sem, osem):
    my = me[0]
    i_move = partner[my] != my

    def load(wait, g):
        part = pl.ds(g * SIZE * C2, SIZE * C2)
        go(recv2.at[part], stage.at[part], sem.at[g], wait)

    def visit(wait, j, moving, rank, p):
        if not wait:
            @pl.when(j % SIZE == 0)
            def _():
                load(True, j // SIZE)

        @pl.when(moving)
        def _():
            own_piece(
                new_in, new_out, rank, NPART, MB2,
                lambda dst: go(stage.at[pl.ds(j * C2 + MA2, MB2)], dst, osem, wait),
            )

        @pl.when(jnp.logical_not(moving))
        def _():
            own_piece(
                new_in, new_out, rank, 0, C2,
                lambda dst: go(stage.at[pl.ds(j * C2, C2)], dst, osem, wait),
            )

    @pl.when(i_move)
    def _():
        copies(partner, nothing, functools.partial(load, False))
        copies(partner, functools.partial(visit, False))
        copies(partner, functools.partial(visit, True))

    @pl.when(jnp.logical_not(i_move))
    def _():
        size = HALF // GROUPS
        pieces = [
            (src.at[pl.ds(g * size, size)], stage.at[pl.ds(h * HALF + g * size, size)],
             dst.at[pl.ds(g * size, size)], g)
            for h, (src, dst) in enumerate(((w_in, new_in), (w_out, new_out)))
            for g in range(GROUPS)
        ]
        for h in range(2):
            half = pieces[h * GROUPS : (h + 1) * GROUPS]
            for src, mid, dst, g in half:
                go(src, mid, sem.at[g], False)
            for src, mid, dst, g in half:
                go(src, mid, sem.at[g], True)
                go(mid, dst, osem, False)
        for src, mid, dst, g in pieces:
            go(mid, dst, osem, True)


def last_kernel(
    me, partner, order, recv3, pos, one, two, gate_one, gate_two, in_, out_,
    res_one, res_two, new_in, new_out, stage, tok, sem, osem, tsem,
):
    my = me[0]
    i_move = partner[my] != my
    go(recv3.at[:, pl.ds(C3, TOK)], tok, tsem, False)

    def load(wait, g):
        part = group_of(g)
        go(recv3.at[part, pl.ds(0, C3)], stage.at[part], sem.at[g], wait)

    @pl.when(i_move)
    def _():
        for g in range(GROUPS):
            load(False, g)

    rows = one.shape[0]
    width = one.shape[1]
    cols = width // 128
    total = 2 * rows
    early = pos[:, 0:1]
    late = pos[:, 1:2]
    lane = lax.broadcasted_iota(jnp.int32, (total, N * 8), 1)
    hot = lambda where: (lane == where).astype(jnp.float32).astype(BF)

    @pl.when(i_move)
    def _():
        for g in range(GROUPS):
            load(True, g)

        def step(k, w, tile):
            go(stage.at[order[k + N // 2]], w.at[pl.ds(tile + C2, C3)], osem, False)
            go(stage.at[order[k]], w.at[pl.ds(tile + NPART + MB2, C3)], osem, False)

        both_halves(step, new_in, new_out)

    go(recv3.at[:, pl.ds(C3, TOK)], tok, tsem, True)
    flat = lambda c: tok[:, c].astype(jnp.float32).reshape(N * 8, 128).astype(BF)
    full = jnp.concatenate([flat(c) for c in range(cols)], axis=1)
    tail = jnp.concatenate([flat(cols + c) for c in range(cols // 2)], axis=1)
    top = jnp.dot(hot(early), full, preferred_element_type=jnp.float32)
    even = jnp.dot(hot(late), tail, preferred_element_type=jnp.float32)
    odd = jnp.dot(
        hot(jnp.where(late < 0, -1, late + 4)), tail, preferred_element_type=jnp.float32
    )
    for b, (group, gate, res) in enumerate(
        ((one, gate_one, res_one), (two, gate_two, res_two))
    ):
        r = slice(b * rows, (b + 1) * rows)
        for c in range(cols):
            s = slice(c * 128, (c + 1) * 128)
            h = slice(c // 2 * 128, (c // 2 + 1) * 128)
            answer = top[r, s] + (odd if c % 2 else even)[r, h]
            res[:, s] = (group[:, s].astype(jnp.float32) + gate[...] * answer).astype(BF)

    @pl.when(i_move)
    def _():
        settled(stage, osem)


def shape(*dims, dtype=BF):
    return jax.ShapeDtypeStruct(dims, dtype)


def exchange(x):
    return lax.all_to_all(x, AXES, split_axis=0, concat_axis=0, tiled=True)


DMA = pltpu.SemaphoreType.DMA(())
SEMS = pltpu.SemaphoreType.DMA((GROUPS,))


def local(
    group_one, routes_one, gates_one, group_two, routes_two, gates_two,
    norm_gain, weight_in, weight_out, old_place, partner,
):
    rows, width = group_one.shape
    ff = weight_in.shape[2]
    me = lax.axis_index(AXES).astype(jnp.int32).reshape(1)
    w_in = tiles_of(weight_in, width, ff)
    w_out = tiles_of(weight_out, ff, width)
    buf1, pos, order = pl.pallas_call(
        first_kernel,
        out_shape=(
            shape(N, C1 + TOK, 8, 128),
            shape(2 * rows, 2, dtype=jnp.int32),
            shape(N, dtype=jnp.int32),
        ),
        in_specs=[SMEM, SMEM, HBM, HBM] + [VMEM] * 6,
        out_specs=(HBM, VMEM, SMEM),
        scratch_shapes=[pltpu.VMEM((N, C1 + TOK, 8, 128), BF), SEMS, DMA],
        name="first",
    )(
        me, partner, w_in, w_out, group_one, group_two,
        routes_one.reshape(1, rows), routes_two.reshape(1, rows),
        norm_gain.reshape(width // 128, 128), old_place.reshape(1, N),
    )
    recv1 = exchange(buf1)
    buf2 = pl.pallas_call(
        second_kernel,
        out_shape=shape(N, C2, 8, 128),
        in_specs=[SMEM, SMEM, SMEM, HBM, HBM, HBM],
        out_specs=HBM,
        scratch_shapes=[pltpu.VMEM((N, C2, 8, 128), BF), SEMS, DMA],
        name="second",
    )(me, partner, order, w_in, w_out, recv1)
    recv2 = exchange(buf2)
    arrived = recv1[:, C1:]
    cols = width // 128
    top = arrived[:, :cols].transpose(0, 2, 1, 3).reshape(N * 8, width)
    rest = arrived[:, cols:].reshape(N, cols // 2, 2, 4, 128)
    rest = rest.transpose(0, 3, 1, 2, 4).reshape(N * 4, width)
    inputs = jnp.concatenate([top, rest], axis=0)
    hidden = jnp.maximum(
        jnp.dot(inputs, weight_in[0], preferred_element_type=jnp.float32), 0.0
    ).astype(BF)
    result = jnp.dot(hidden, weight_out[0], preferred_element_type=jnp.float32).astype(BF)
    top = result[: N * 8].reshape(N, 8, cols, 128).transpose(0, 2, 1, 3)
    rest = result[N * 8 :].reshape(N, 4, cols // 2, 2, 128)
    rest = rest.transpose(0, 2, 3, 1, 4).reshape(N, cols // 2, 8, 128)
    answers = jnp.concatenate([top, rest], axis=1)
    buf3 = pl.pallas_call(
        third_kernel,
        out_shape=shape(N, C3 + TOK, 8, 128),
        in_specs=[SMEM, SMEM, SMEM, HBM, HBM, HBM],
        out_specs=HBM,
        scratch_shapes=[
            pltpu.VMEM((N // 2, C3, 8, 128), BF), pltpu.VMEM((N, TOK, 8, 128), BF), SEMS, DMA, DMA,
        ],
        name="third",
    )(me, partner, order, recv1, recv2, answers)
    recv3 = exchange(buf3)
    new_in, new_out = pl.pallas_call(
        settle_kernel,
        out_shape=(shape(HALF, 8, 128), shape(HALF, 8, 128)),
        in_specs=[SMEM, SMEM, HBM, HBM, HBM],
        out_specs=(HBM, HBM),
        scratch_shapes=[pltpu.VMEM((2 * HALF, 8, 128), BF), SEMS, DMA],
        name="settle",
    )(me, partner, w_in, w_out, recv2.reshape(N * C2, 8, 128))
    res_one, res_two, new_in, new_out = pl.pallas_call(
        last_kernel,
        out_shape=(
            shape(rows, width), shape(rows, width), shape(HALF, 8, 128), shape(HALF, 8, 128),
        ),
        in_specs=[SMEM, SMEM, SMEM, HBM] + [VMEM] * 5 + [HBM, HBM],
        out_specs=(VMEM, VMEM, HBM, HBM),
        scratch_shapes=[
            pltpu.VMEM((N, C3, 8, 128), BF), pltpu.VMEM((N, TOK, 8, 128), BF), SEMS, DMA, DMA,
        ],
        input_output_aliases={9: 2, 10: 3},
        name="last",
    )(
        me, partner, order, recv3, pos, group_one, group_two,
        gates_one.reshape(rows, 1), gates_two.reshape(rows, 1), new_in, new_out,
    )
    return (res_one, res_two, array_of(new_in, width, ff), array_of(new_out, ff, width))


def solution(mesh):
    split = P(AXES, None)
    flat = P(AXES)
    deep = P(AXES, None, None)
    return jax.shard_map(
        local,
        mesh=mesh,
        in_specs=(split, split, flat, split, split, flat, P(), deep, deep, P(), P()),
        out_specs=(split, split, deep, deep),
        check_vma=False,
    )
```

```python
import functools

import jax
import jax.numpy as jnp
from jax import lax
from jax.experimental import pallas as pl
from jax.experimental.pallas import tpu as pltpu
from jax.sharding import PartitionSpec as P

AXES = ("gx", "gy")
EPS = 1e-06
CAP = 6
N = 128
HALF = 2304
CHUNK = 72
TOK = 9
C1, C2, C3 = 21, 20, 21
NPART = 41
MA2 = 10
MB2 = C2 - MA2
GROUPS = 8
SIZE = N // GROUPS
UNROLL = 4

HBM = pl.BlockSpec(memory_space=pltpu.MemorySpace.HBM)
SMEM = pl.BlockSpec(memory_space=pltpu.SMEM)
VMEM = pl.BlockSpec(memory_space=pltpu.VMEM)
BF = jnp.bfloat16


def tiles_of(w, rows, cols):
    return w.reshape(rows // 8, 8, cols // 128, 128).transpose(0, 2, 1, 3).reshape(HALF, 8, 128)


def array_of(t, rows, cols):
    return t.reshape(rows // 8, cols // 128, 8, 128).transpose(0, 2, 1, 3).reshape(1, rows, cols)


def copies(partner, visit, after=None):
    def step(j, counts):
        movers, stayers = counts
        p = partner[j]
        moving = p != j
        visit(j, moving, jnp.where(moving, movers, stayers), p)
        one = moving.astype(jnp.int32)
        return (movers + one, stayers + 1 - one)

    def group(g, counts):
        counts = lax.fori_loop(g * SIZE, (g + 1) * SIZE, step, counts)
        if after is not None:
            after(g)
        return counts

    lax.fori_loop(0, GROUPS, group, (jnp.int32(0), jnp.int32(0)))


def own_piece(w_in, w_out, rank, offset, size, act):
    @pl.when(rank < 32)
    def _():
        act(w_in.at[pl.ds(rank * CHUNK + offset, size)])

    @pl.when(rank >= 32)
    def _():
        act(w_out.at[pl.ds((rank - 32) * CHUNK + offset, size)])


def go(src, dst, sem, wait):
    copy = pltpu.make_async_copy(src, dst, sem)
    if wait:
        copy.wait()
    else:
        copy.start()


def nothing(j, moving, rank, p):
    pass


def column(row):
    n = row.shape[1]
    eye = lax.broadcasted_iota(jnp.int32, (n, n), 0) == lax.broadcasted_iota(jnp.int32, (n, n), 1)
    return jnp.sum(jnp.where(eye, row, 0), axis=1, keepdims=True)


def both_halves(step, w_in, w_out):
    half = N // 4
    lax.fori_loop(0, half, lambda k, c: (step(k, w_in, k * CHUNK), c)[1], 0, unroll=UNROLL)
    lax.fori_loop(
        0, half, lambda k, c: (step(k + half, w_out, k * CHUNK), c)[1], 0, unroll=UNROLL
    )


def each_mover(step):
    lax.fori_loop(0, N // 2, lambda k, c: (step(k), c)[1], 0, unroll=UNROLL)


def settled(ref, sem):
    pltpu.make_async_copy(ref, ref, sem).wait()


def group_of(g):
    return pl.ds(g * SIZE, SIZE)


def first_kernel(
    me, partner, w_in, w_out, *refs,
):
    given, (buf1, pos_out, order, stage, *held, pos, sem, osem, isem) = refs[:6], refs[6:]
    one, two, routes_one, routes_two, gain, place = held
    my = me[0]
    i_move = partner[my] != my
    for src, dst in zip(given, held):
        go(src, dst, isem, False)

    def sort(j, counts):
        movers, stayers = counts
        moving = partner[j] != j
        order[jnp.where(moving, movers, stayers)] = j
        one = moving.astype(jnp.int32)
        return (movers + one, stayers + 1 - one)

    lax.fori_loop(0, N, sort, (jnp.int32(0), jnp.int32(N // 2)), unroll=UNROLL)

    @pl.when(i_move)
    def _():
        def step(k, w, tile):
            m = order[k]
            t = order[k + N // 2]
            go(w.at[pl.ds(tile, C1)], stage.at[t, pl.ds(0, C1)], sem.at[t // SIZE], False)
            go(w.at[pl.ds(tile + NPART, C1)], stage.at[m, pl.ds(0, C1)], sem.at[m // SIZE], False)

        both_halves(step, w_in, w_out)

    rows = one.shape[0]
    width = one.shape[1]
    cols = width // 128
    total = 2 * rows
    for src, dst in zip(given, held):
        go(src, dst, isem, True)
    slots = place[...]
    lower = (
        lax.broadcasted_iota(jnp.int32, (rows, rows), 1)
        < lax.broadcasted_iota(jnp.int32, (rows, rows), 0)
    ).astype(jnp.float32).astype(BF)
    lane = lax.broadcasted_iota(jnp.int32, (rows, N), 1)
    scale = jnp.concatenate([gain[c : c + 1, :] for c in range(cols)], axis=1)
    normed, target, place_in = [], [], []
    for b, (group, routes) in enumerate(((one, routes_one), (two, routes_two))):
        values = group[...].astype(jnp.float32)
        scaling = lax.rsqrt(jnp.mean(values * values, axis=1, keepdims=True) + EPS)
        normed.append((values * scaling * scale).astype(BF))
        member = column(routes[...]) == slots
        flag = member.astype(jnp.float32)
        before = jnp.dot(lower, flag.astype(BF), preferred_element_type=jnp.float32)
        target.append(jnp.sum(jnp.where(member, lane, 0), axis=1, keepdims=True))
        place_in.append(
            jnp.sum(flag * before, axis=1, keepdims=True).astype(jnp.int32) + b * CAP
        )
    normed = jnp.concatenate(normed, axis=0)
    target = jnp.concatenate(target, axis=0)
    place_in = jnp.concatenate(place_in, axis=0)
    early = jnp.where(place_in < 8, target * 8 + place_in, -1)
    late = jnp.where(place_in < 8, -1, target * 8 + place_in - 8)
    pos[:, 0:1] = early
    pos[:, 1:2] = late
    go(pos, pos_out, isem, False)

    def tiles(lo, size):
        go(stage.at[:, pl.ds(lo, size)], buf1.at[:, pl.ds(lo, size)], osem, False)

    def out(lo, size, g):
        part = group_of(g)
        go(stage.at[part, pl.ds(lo, size)], buf1.at[part, pl.ds(lo, size)], osem, False)

    @pl.when(i_move)
    def _():
        for g in range(GROUPS):
            settled(stage.at[group_of(g), pl.ds(0, C1)], sem.at[g])
            out(0, C1, g)

    eye = lax.broadcasted_iota(jnp.int32, (total, total), 0) == lax.broadcasted_iota(
        jnp.int32, (total, total), 1
    )
    early_row = jnp.sum(jnp.where(eye, early, 0), axis=0, keepdims=True)
    late_row = jnp.sum(jnp.where(eye, late, 0), axis=0, keepdims=True)
    row = lax.broadcasted_iota(jnp.int32, (N * 8, total), 0)
    fours = row - (row & 4)
    upper = lax.broadcasted_iota(jnp.int32, (N, 8, 128), 1) < 4
    cut = lambda x, c: x[:, c * 128 : (c + 1) * 128].reshape(N, 8, 128)
    pick = (fours == late_row).astype(jnp.float32).astype(BF)
    rest = jnp.dot(pick, normed, preferred_element_type=jnp.float32)
    for c in range(cols // 2):
        stage[:, C1 + cols + c] = jnp.where(upper, cut(rest, 2 * c), cut(rest, 2 * c + 1)).astype(BF)
    tiles(C1 + cols, cols // 2)
    pick = (row == early_row).astype(jnp.float32).astype(BF)
    top = jnp.dot(pick, normed, preferred_element_type=jnp.float32)
    for c in range(cols):
        stage[:, C1 + c] = cut(top, c).astype(BF)
    tiles(C1, cols)
    go(pos, pos_out, isem, True)
    settled(stage.at[:, pl.ds(C1, TOK)], osem)

    @pl.when(i_move)
    def _():
        settled(stage.at[:, pl.ds(0, C1)], osem)


def second_own_kernel(me, partner, order, w_in, w_out, buf2, stage, sem, osem):
    my = me[0]

    @pl.when(partner[my] != my)
    def _():
        def step(k, w, tile):
            m = order[k]
            t = order[k + N // 2]
            at = sem.at[k // SIZE]
            go(w.at[pl.ds(tile + C1, C2)], stage.at[k, pl.ds(0, C2)], at, False)
            go(w.at[pl.ds(tile + NPART + C1, MA2)], stage.at[k, pl.ds(C2, MA2)], at, False)

        both_halves(step, w_in, w_out)
        for g in range(N // 2 // SIZE):
            settled(stage.at[group_of(g)], sem.at[g])

            def send(i, c):
                k = g * SIZE + i
                m = order[k]
                t = order[k + N // 2]
                go(stage.at[k, pl.ds(0, C2)], buf2.at[t], osem, False)
                go(stage.at[k, pl.ds(C2, MA2)], buf2.at[m, pl.ds(0, MA2)], osem, False)
                return c

            lax.fori_loop(0, SIZE, send, 0, unroll=UNROLL)
        settled(stage, osem)


def forward_kernel(of_mover, of_stayer, tokens, me, partner, order, recv, *refs):
    my = me[0]
    i_move = partner[my] != my
    if tokens:
        answers, buf, stage, tok, sem, osem, tsem = refs
        go(answers, tok, tsem, False)
    else:
        _, buf, stage, sem, osem = refs

    def between():
        if tokens:
            go(answers, tok, tsem, True)
            go(tok, buf.at[:, pl.ds(C3, TOK)], tsem, False)

    for mine, piece in ((True, of_mover), (False, of_stayer)):
        @pl.when(i_move == mine)
        def _():
            forward(order, partner, stage, buf, sem, osem, recv, *piece, between)

    if tokens:
        go(tok, buf.at[:, pl.ds(C3, TOK)], tsem, True)


def forward(order, partner, stage, buf, sem, osem, recv, lo, to, size, between):
    groups = N // 2 // SIZE

    def load(k):
        p = partner[order[k]]
        go(recv.at[p, pl.ds(lo, size)], stage.at[k, pl.ds(0, size)], sem.at[k // SIZE], False)

    each_mover(load)
    between()
    for g in range(groups):
        settled(stage.at[group_of(g), pl.ds(0, size)], sem.at[g])

        def send(i, c):
            k = g * SIZE + i
            go(stage.at[k, pl.ds(0, size)], buf.at[order[k], pl.ds(to, size)], osem, False)
            return c

        lax.fori_loop(0, SIZE, send, 0, unroll=UNROLL)
    settled(stage.at[pl.ds(0, N // 2), pl.ds(0, size)], osem)


def settle_kernel(me, partner, w_in, w_out, recv2, new_in, new_out, stage, sem, osem):
    my = me[0]
    i_move = partner[my] != my

    def load(wait, g):
        part = pl.ds(g * SIZE * C2, SIZE * C2)
        go(recv2.at[part], stage.at[part], sem.at[g], wait)

    def visit(wait, j, moving, rank, p):
        if not wait:
            @pl.when(j % SIZE == 0)
            def _():
                load(True, j // SIZE)

        @pl.when(moving)
        def _():
            own_piece(
                new_in, new_out, rank, NPART, MB2,
                lambda dst: go(stage.at[pl.ds(j * C2 + MA2, MB2)], dst, osem, wait),
            )

        @pl.when(jnp.logical_not(moving))
        def _():
            own_piece(
                new_in, new_out, rank, 0, C2,
                lambda dst: go(stage.at[pl.ds(j * C2, C2)], dst, osem, wait),
            )

    @pl.when(i_move)
    def _():
        copies(partner, nothing, functools.partial(load, False))
        copies(partner, functools.partial(visit, False))
        copies(partner, functools.partial(visit, True))

    @pl.when(jnp.logical_not(i_move))
    def _():
        size = HALF // GROUPS
        pieces = [
            (src.at[pl.ds(g * size, size)], stage.at[pl.ds(h * HALF + g * size, size)],
             dst.at[pl.ds(g * size, size)], g)
            for h, (src, dst) in enumerate(((w_in, new_in), (w_out, new_out)))
            for g in range(GROUPS)
        ]
        for h in range(2):
            half = pieces[h * GROUPS : (h + 1) * GROUPS]
            for src, mid, dst, g in half:
                go(src, mid, sem.at[g], False)
            for src, mid, dst, g in half:
                go(src, mid, sem.at[g], True)
                go(mid, dst, osem, False)
        for src, mid, dst, g in pieces:
            go(mid, dst, osem, True)


def last_kernel(
    me, partner, order, recv3, *refs,
):
    given, (in_, out_, *results, new_in, new_out) = refs[:5], refs[5:11]
    stage, tok, *held, res_one, res_two, sem, osem, tsem, isem = refs[11:]
    pos, one, two, gate_one, gate_two = held
    my = me[0]
    i_move = partner[my] != my
    go(recv3.at[:, pl.ds(C3, TOK)], tok, tsem, False)

    def load(wait, g):
        part = group_of(g)
        go(recv3.at[part, pl.ds(0, C3)], stage.at[part], sem.at[g], wait)

    @pl.when(i_move)
    def _():
        for g in range(GROUPS):
            load(False, g)

    for src, dst in zip(given, held):
        go(src, dst, isem, False)
    rows = one.shape[0]
    width = one.shape[1]
    cols = width // 128
    total = 2 * rows
    for src, dst in zip(given, held):
        go(src, dst, isem, True)
    early = pos[:, 0:1]
    late = pos[:, 1:2]
    lane = lax.broadcasted_iota(jnp.int32, (total, N * 8), 1)
    hot = lambda where: (lane == where).astype(jnp.float32).astype(BF)

    @pl.when(i_move)
    def _():
        for g in range(GROUPS):
            load(True, g)

        def step(k, w, tile):
            go(stage.at[order[k + N // 2]], w.at[pl.ds(tile + C2, C3)], osem, False)
            go(stage.at[order[k]], w.at[pl.ds(tile + NPART + MB2, C3)], osem, False)

        both_halves(step, new_in, new_out)

    go(recv3.at[:, pl.ds(C3, TOK)], tok, tsem, True)
    flat = lambda c: tok[:, c].astype(jnp.float32).reshape(N * 8, 128).astype(BF)
    full = jnp.concatenate([flat(c) for c in range(cols)], axis=1)
    tail = jnp.concatenate([flat(cols + c) for c in range(cols // 2)], axis=1)
    top = jnp.dot(hot(early), full, preferred_element_type=jnp.float32)
    even = jnp.dot(hot(late), tail, preferred_element_type=jnp.float32)
    odd = jnp.dot(
        hot(jnp.where(late < 0, -1, late + 4)), tail, preferred_element_type=jnp.float32
    )
    for b, (group, gate, res) in enumerate(
        ((one, gate_one, res_one), (two, gate_two, res_two))
    ):
        r = slice(b * rows, (b + 1) * rows)
        for c in range(cols):
            s = slice(c * 128, (c + 1) * 128)
            h = slice(c // 2 * 128, (c // 2 + 1) * 128)
            answer = top[r, s] + (odd if c % 2 else even)[r, h]
            res[:, s] = (group[:, s].astype(jnp.float32) + gate[...] * answer).astype(BF)
        go(res, results[b], isem, False)
    for b, res in enumerate((res_one, res_two)):
        go(res, results[b], isem, True)

    @pl.when(i_move)
    def _():
        settled(stage, osem)


def shape(*dims, dtype=BF):
    return jax.ShapeDtypeStruct(dims, dtype)


def exchange(x):
    return lax.all_to_all(x, AXES, split_axis=0, concat_axis=0, tiled=True)


DMA = pltpu.SemaphoreType.DMA(())
SEMS = pltpu.SemaphoreType.DMA((GROUPS,))


def local(
    group_one, routes_one, gates_one, group_two, routes_two, gates_two,
    norm_gain, weight_in, weight_out, old_place, partner,
):
    rows, width = group_one.shape
    ff = weight_in.shape[2]
    me = lax.axis_index(AXES).astype(jnp.int32).reshape(1)
    w_in = tiles_of(weight_in, width, ff)
    w_out = tiles_of(weight_out, ff, width)
    buf1, pos, order = pl.pallas_call(
        first_kernel,
        out_shape=(
            shape(N, C1 + TOK, 8, 128),
            shape(2 * rows, 2, dtype=jnp.int32),
            shape(N, dtype=jnp.int32),
        ),
        in_specs=[SMEM, SMEM, HBM, HBM] + [HBM] * 6,
        out_specs=(HBM, HBM, SMEM),
        scratch_shapes=[
            pltpu.VMEM((N, C1 + TOK, 8, 128), BF),
            pltpu.VMEM((rows, width), BF), pltpu.VMEM((rows, width), BF),
            pltpu.VMEM((1, rows), jnp.int32), pltpu.VMEM((1, rows), jnp.int32),
            pltpu.VMEM((width // 128, 128), jnp.float32), pltpu.VMEM((1, N), jnp.int32),
            pltpu.VMEM((2 * rows, 2), jnp.int32), SEMS, DMA, DMA,
        ],
        name="first",
    )(
        me, partner, w_in, w_out, group_one, group_two,
        routes_one.reshape(1, rows), routes_two.reshape(1, rows),
        norm_gain.reshape(width // 128, 128), old_place.reshape(1, N),
    )
    recv1 = exchange(buf1)
    buf2 = pl.pallas_call(
        second_own_kernel,
        out_shape=shape(N, C2, 8, 128),
        in_specs=[SMEM, SMEM, SMEM, HBM, HBM],
        out_specs=HBM,
        scratch_shapes=[pltpu.VMEM((N // 2, C2 + MA2, 8, 128), BF), SEMS, DMA],
        name="second_own",
    )(me, partner, order, w_in, w_out)
    buf2 = pl.pallas_call(
        functools.partial(forward_kernel, (0, MA2, MB2), (0, 0, C2), False),
        out_shape=shape(N, C2, 8, 128),
        in_specs=[SMEM, SMEM, SMEM, HBM, HBM],
        out_specs=HBM,
        scratch_shapes=[pltpu.VMEM((N // 2, C2, 8, 128), BF), SEMS, DMA],
        input_output_aliases={4: 0},
        name="second_forward",
    )(me, partner, order, recv1, buf2)
    recv2 = exchange(buf2)
    arrived = recv1[:, C1:]
    cols = width // 128
    top = arrived[:, :cols].transpose(0, 2, 1, 3).reshape(N * 8, width)
    rest = arrived[:, cols:].reshape(N, cols // 2, 2, 4, 128)
    rest = rest.transpose(0, 3, 1, 2, 4).reshape(N * 4, width)
    inputs = jnp.concatenate([top, rest], axis=0)
    hidden = jnp.maximum(
        jnp.dot(inputs, weight_in[0], preferred_element_type=jnp.float32), 0.0
    ).astype(BF)
    result = jnp.dot(hidden, weight_out[0], preferred_element_type=jnp.float32).astype(BF)
    top = result[: N * 8].reshape(N, 8, cols, 128).transpose(0, 2, 1, 3)
    rest = result[N * 8 :].reshape(N, 4, cols // 2, 2, 128)
    rest = rest.transpose(0, 2, 3, 1, 4).reshape(N, cols // 2, 8, 128)
    answers = jnp.concatenate([top, rest], axis=1)
    buf3 = pl.pallas_call(
        functools.partial(forward_kernel, (MB2, 0, C1 - MB2), (C2, 0, C1 - C2), True),
        out_shape=shape(N, C3 + TOK, 8, 128),
        in_specs=[SMEM, SMEM, SMEM, HBM, HBM],
        out_specs=HBM,
        scratch_shapes=[
            pltpu.VMEM((N // 2, C1 - MB2, 8, 128), BF), pltpu.VMEM((N, TOK, 8, 128), BF),
            SEMS, DMA, DMA,
        ],
        name="third_held",
    )(me, partner, order, recv1, answers)
    buf3 = pl.pallas_call(
        functools.partial(forward_kernel, (0, C1 - MB2, MA2), (0, C1 - C2, C2), False),
        out_shape=shape(N, C3 + TOK, 8, 128),
        in_specs=[SMEM, SMEM, SMEM, HBM, HBM],
        out_specs=HBM,
        scratch_shapes=[pltpu.VMEM((N // 2, C2, 8, 128), BF), SEMS, DMA],
        input_output_aliases={4: 0},
        name="third_forward",
    )(me, partner, order, recv2, buf3)
    recv3 = exchange(buf3)
    new_in, new_out = pl.pallas_call(
        settle_kernel,
        out_shape=(shape(HALF, 8, 128), shape(HALF, 8, 128)),
        in_specs=[SMEM, SMEM, HBM, HBM, HBM],
        out_specs=(HBM, HBM),
        scratch_shapes=[pltpu.VMEM((2 * HALF, 8, 128), BF), SEMS, DMA],
        name="settle",
    )(me, partner, w_in, w_out, recv2.reshape(N * C2, 8, 128))
    res_one, res_two, new_in, new_out = pl.pallas_call(
        last_kernel,
        out_shape=(
            shape(rows, width), shape(rows, width), shape(HALF, 8, 128), shape(HALF, 8, 128),
        ),
        in_specs=[SMEM, SMEM, SMEM, HBM] + [HBM] * 7,
        out_specs=(HBM, HBM, HBM, HBM),
        scratch_shapes=[
            pltpu.VMEM((N, C3, 8, 128), BF), pltpu.VMEM((N, TOK, 8, 128), BF),
            pltpu.VMEM((2 * rows, 2), jnp.int32),
            pltpu.VMEM((rows, width), BF), pltpu.VMEM((rows, width), BF),
            pltpu.VMEM((rows, 1), jnp.float32), pltpu.VMEM((rows, 1), jnp.float32),
            pltpu.VMEM((rows, width), BF), pltpu.VMEM((rows, width), BF),
            SEMS, DMA, DMA, DMA,
        ],
        input_output_aliases={9: 2, 10: 3},
        name="last",
    )(
        me, partner, order, recv3, pos, group_one, group_two,
        gates_one.reshape(rows, 1), gates_two.reshape(rows, 1), new_in, new_out,
    )
    return (res_one, res_two, array_of(new_in, width, ff), array_of(new_out, ff, width))


def solution(mesh):
    split = P(AXES, None)
    flat = P(AXES)
    deep = P(AXES, None, None)
    return jax.shard_map(
        local,
        mesh=mesh,
        in_specs=(split, split, flat, split, split, flat, P(), deep, deep, P(), P()),
        out_specs=(split, split, deep, deep),
        check_vma=False,
    )
```

```python
import functools

import jax
import jax.numpy as jnp
from jax import lax
from jax.experimental import pallas as pl
from jax.experimental.pallas import tpu as pltpu
from jax.sharding import PartitionSpec as P

AXES = ("gx", "gy")
EPS = 1e-06
CAP = 6
N = 128
HALF = 2304
CHUNK = 72
TOK = 9
C1, C2, C3 = 21, 20, 21
NPART = 41
MA2 = 10
MB2 = C2 - MA2
GROUPS = 8
SIZE = N // GROUPS
UNROLL = 4
FEW = 8

HBM = pl.BlockSpec(memory_space=pltpu.MemorySpace.HBM)
SMEM = pl.BlockSpec(memory_space=pltpu.SMEM)
VMEM = pl.BlockSpec(memory_space=pltpu.VMEM)
BF = jnp.bfloat16


def tiles_of(w, rows, cols):
    return w.reshape(rows // 8, 8, cols // 128, 128).transpose(0, 2, 1, 3).reshape(HALF, 8, 128)


def array_of(t, rows, cols):
    return t.reshape(rows // 8, cols // 128, 8, 128).transpose(0, 2, 1, 3).reshape(1, rows, cols)


def go(src, dst, sem, wait):
    copy = pltpu.make_async_copy(src, dst, sem)
    if wait:
        copy.wait()
    else:
        copy.start()


def column(row):
    n = row.shape[1]
    eye = lax.broadcasted_iota(jnp.int32, (n, n), 0) == lax.broadcasted_iota(jnp.int32, (n, n), 1)
    return jnp.sum(jnp.where(eye, row, 0), axis=1, keepdims=True)


def both_halves(step, w_in, w_out):
    half = N // 4
    lax.fori_loop(0, half, lambda k, c: (step(k, w_in, k * CHUNK), c)[1], 0, unroll=UNROLL)
    lax.fori_loop(
        0, half, lambda k, c: (step(k + half, w_out, k * CHUNK), c)[1], 0, unroll=UNROLL
    )


def each_mover(step):
    lax.fori_loop(0, N // 2, lambda k, c: (step(k), c)[1], 0, unroll=UNROLL)


def settled(ref, sem):
    pltpu.make_async_copy(ref, ref, sem).wait()


def group_of(g):
    return pl.ds(g * SIZE, SIZE)


def first_kernel(
    me, partner, w_in, w_out, *refs,
):
    given, (buf1, pos_out, order, stage, *held, pos, sem, osem, isem) = refs[:6], refs[6:]
    one, two, routes_one, routes_two, gain, place = held
    my = me[0]
    i_move = partner[my] != my
    for src, dst in zip(given, held):
        go(src, dst, isem, False)

    def sort(j, counts):
        movers, stayers = counts
        moving = partner[j] != j
        order[jnp.where(moving, movers, stayers)] = j
        one = moving.astype(jnp.int32)
        return (movers + one, stayers + 1 - one)

    lax.fori_loop(0, N, sort, (jnp.int32(0), jnp.int32(N // 2)), unroll=UNROLL)

    @pl.when(i_move)
    def _():
        def step(k, w, tile):
            m = order[k]
            t = order[k + N // 2]
            go(w.at[pl.ds(tile, C1)], stage.at[t, pl.ds(0, C1)], sem.at[t // SIZE], False)
            go(w.at[pl.ds(tile + NPART, C1)], stage.at[m, pl.ds(0, C1)], sem.at[m // SIZE], False)

        both_halves(step, w_in, w_out)

    rows = one.shape[0]
    width = one.shape[1]
    cols = width // 128
    total = 2 * rows
    for src, dst in zip(given, held):
        go(src, dst, isem, True)
    slots = place[...]
    lower = (
        lax.broadcasted_iota(jnp.int32, (rows, rows), 1)
        < lax.broadcasted_iota(jnp.int32, (rows, rows), 0)
    ).astype(jnp.float32).astype(BF)
    lane = lax.broadcasted_iota(jnp.int32, (rows, N), 1)
    scale = jnp.concatenate([gain[c : c + 1, :] for c in range(cols)], axis=1)
    normed, target, place_in = [], [], []
    for b, (group, routes) in enumerate(((one, routes_one), (two, routes_two))):
        values = group[...].astype(jnp.float32)
        scaling = lax.rsqrt(jnp.mean(values * values, axis=1, keepdims=True) + EPS)
        normed.append((values * scaling * scale).astype(BF))
        member = column(routes[...]) == slots
        flag = member.astype(jnp.float32)
        before = jnp.dot(lower, flag.astype(BF), preferred_element_type=jnp.float32)
        target.append(jnp.sum(jnp.where(member, lane, 0), axis=1, keepdims=True))
        place_in.append(
            jnp.sum(flag * before, axis=1, keepdims=True).astype(jnp.int32) + b * CAP
        )
    normed = jnp.concatenate(normed, axis=0)
    target = jnp.concatenate(target, axis=0)
    place_in = jnp.concatenate(place_in, axis=0)
    early = jnp.where(place_in < 8, target * 8 + place_in, -1)
    late = jnp.where(place_in < 8, -1, target * 8 + place_in - 8)
    pos[:, 0:1] = early
    pos[:, 1:2] = late
    go(pos, pos_out, isem, False)

    def tiles(lo, size):
        go(stage.at[:, pl.ds(lo, size)], buf1.at[:, pl.ds(lo, size)], osem, False)

    def out(lo, size, g):
        part = group_of(g)
        go(stage.at[part, pl.ds(lo, size)], buf1.at[part, pl.ds(lo, size)], osem, False)

    @pl.when(i_move)
    def _():
        for g in range(GROUPS):
            settled(stage.at[group_of(g), pl.ds(0, C1)], sem.at[g])
            out(0, C1, g)

    eye = lax.broadcasted_iota(jnp.int32, (total, total), 0) == lax.broadcasted_iota(
        jnp.int32, (total, total), 1
    )
    early_row = jnp.sum(jnp.where(eye, early, 0), axis=0, keepdims=True)
    late_row = jnp.sum(jnp.where(eye, late, 0), axis=0, keepdims=True)
    row = lax.broadcasted_iota(jnp.int32, (N * 8, total), 0)
    fours = row - (row & 4)
    upper = lax.broadcasted_iota(jnp.int32, (N, 8, 128), 1) < 4
    cut = lambda x, c: x[:, c * 128 : (c + 1) * 128].reshape(N, 8, 128)
    pick = (fours == late_row).astype(jnp.float32).astype(BF)
    rest = jnp.dot(pick, normed, preferred_element_type=jnp.float32)
    for c in range(cols // 2):
        stage[:, C1 + cols + c] = jnp.where(upper, cut(rest, 2 * c), cut(rest, 2 * c + 1)).astype(BF)
    tiles(C1 + cols, cols // 2)
    pick = (row == early_row).astype(jnp.float32).astype(BF)
    top = jnp.dot(pick, normed, preferred_element_type=jnp.float32)
    for c in range(cols):
        stage[:, C1 + c] = cut(top, c).astype(BF)
    tiles(C1, cols)
    go(pos, pos_out, isem, True)
    settled(stage.at[:, pl.ds(C1, TOK)], osem)

    @pl.when(i_move)
    def _():
        settled(stage.at[:, pl.ds(0, C1)], osem)


def in_turn(w_in, w_out, act):
    half = N // 4
    for w, start in ((w_in, 0), (w_out, half)):
        lax.fori_loop(
            0, half // FEW, lambda g, c: (act(start + g * FEW, w, g * FEW * CHUNK), c)[1], 0
        )


def second_own_kernel(me, partner, order, w_in, w_out, buf2, stage, sem, osem):
    my = me[0]

    def act(first, w, base):
        for i in range(FEW):
            tile = base + i * CHUNK
            go(w.at[pl.ds(tile + C1, C2)], stage.at[i, pl.ds(0, C2)], sem, False)
            go(w.at[pl.ds(tile + NPART + C1, MA2)], stage.at[i, pl.ds(C2, MA2)], sem, False)
        settled(stage, sem)
        for i in range(FEW):
            m = order[first + i]
            t = order[first + i + N // 2]
            go(stage.at[i, pl.ds(0, C2)], buf2.at[t], osem, False)
            go(stage.at[i, pl.ds(C2, MA2)], buf2.at[m, pl.ds(0, MA2)], osem, False)
        settled(stage, osem)

    @pl.when(partner[my] != my)
    def _():
        in_turn(w_in, w_out, act)


def forward_kernel(of_mover, of_stayer, tokens, me, partner, order, recv, *refs):
    my = me[0]
    i_move = partner[my] != my
    if tokens:
        answers, buf, stage, tok, sem, osem, tsem = refs
        go(answers, tok, tsem, False)
    else:
        _, buf, stage, sem, osem = refs

    def between():
        if tokens:
            go(answers, tok, tsem, True)
            go(tok, buf.at[:, pl.ds(C3, TOK)], tsem, False)

    for mine, piece in ((True, of_mover), (False, of_stayer)):
        @pl.when(i_move == mine)
        def _():
            forward(order, partner, stage, buf, sem, osem, recv, *piece, tokens, between)

    if tokens:
        go(tok, buf.at[:, pl.ds(C3, TOK)], tsem, True)


def forward(order, partner, stage, buf, sem, osem, recv, lo, to, size, slow, between):
    groups = N // 2 // SIZE

    def load(k):
        p = partner[order[k]]
        go(recv.at[p, pl.ds(lo, size)], stage.at[k, pl.ds(0, size)], sem.at[k // SIZE], False)

    if slow:
        between()
    else:
        each_mover(load)
    for g in range(groups):
        if slow:
            for i in range(SIZE):
                load(g * SIZE + i)
        settled(stage.at[group_of(g), pl.ds(0, size)], sem.at[g])

        def send(i, c):
            k = g * SIZE + i
            go(stage.at[k, pl.ds(0, size)], buf.at[order[k], pl.ds(to, size)], osem, False)
            return c

        lax.fori_loop(0, SIZE, send, 0, unroll=UNROLL)
        if slow:
            settled(stage.at[group_of(g), pl.ds(0, size)], osem)
    if not slow:
        settled(stage.at[pl.ds(0, N // 2), pl.ds(0, size)], osem)


def settle_kernel(
    me, partner, order, w_in, w_out, recv2, new_in, new_out, stage, whole, sem, osem
):
    my = me[0]
    i_move = partner[my] != my

    def act(first, w, base):
        for i in range(FEW):
            m = order[first + i]
            t = order[first + i + N // 2]
            go(recv2.at[t], stage.at[i, pl.ds(0, C2)], sem, False)
            go(recv2.at[m, pl.ds(MA2, MB2)], stage.at[i, pl.ds(C2, MB2)], sem, False)
        settled(stage, sem)
        for i in range(FEW):
            tile = base + i * CHUNK
            go(stage.at[i, pl.ds(0, C2)], w.at[pl.ds(tile, C2)], osem, False)
            go(stage.at[i, pl.ds(C2, MB2)], w.at[pl.ds(tile + NPART, MB2)], osem, False)
        settled(stage, osem)

    @pl.when(i_move)
    def _():
        in_turn(new_in, new_out, act)

    @pl.when(jnp.logical_not(i_move))
    def _():
        size = whole.shape[0]
        for src, dst in ((w_in, new_in), (w_out, new_out)):
            def step(g, c):
                part = pl.ds(g * size, size)
                go(src.at[part], whole, sem, False)
                go(src.at[part], whole, sem, True)
                go(whole, dst.at[part], osem, False)
                go(whole, dst.at[part], osem, True)
                return c

            lax.fori_loop(0, HALF // size, step, 0)


def last_kernel(
    me, partner, order, recv3, *refs,
):
    given, (in_, out_, *results, new_in, new_out) = refs[:5], refs[5:11]
    stage, tok, *held, res_one, res_two, sem, osem, tsem, isem = refs[11:]
    pos, one, two, gate_one, gate_two = held
    my = me[0]
    i_move = partner[my] != my
    go(recv3.at[:, pl.ds(C3, TOK)], tok, tsem, False)

    def load(wait, g):
        part = group_of(g)
        go(recv3.at[part, pl.ds(0, C3)], stage.at[part], sem.at[g], wait)

    @pl.when(i_move)
    def _():
        for g in range(GROUPS):
            load(False, g)

    for src, dst in zip(given, held):
        go(src, dst, isem, False)
    rows = one.shape[0]
    width = one.shape[1]
    cols = width // 128
    total = 2 * rows
    for src, dst in zip(given, held):
        go(src, dst, isem, True)
    early = pos[:, 0:1]
    late = pos[:, 1:2]
    lane = lax.broadcasted_iota(jnp.int32, (total, N * 8), 1)
    hot = lambda where: (lane == where).astype(jnp.float32).astype(BF)

    @pl.when(i_move)
    def _():
        for g in range(GROUPS):
            load(True, g)

        def step(k, w, tile):
            go(stage.at[order[k + N // 2]], w.at[pl.ds(tile + C2, C3)], osem, False)
            go(stage.at[order[k]], w.at[pl.ds(tile + NPART + MB2, C3)], osem, False)

        both_halves(step, new_in, new_out)

    go(recv3.at[:, pl.ds(C3, TOK)], tok, tsem, True)
    flat = lambda c: tok[:, c].astype(jnp.float32).reshape(N * 8, 128).astype(BF)
    full = jnp.concatenate([flat(c) for c in range(cols)], axis=1)
    tail = jnp.concatenate([flat(cols + c) for c in range(cols // 2)], axis=1)
    top = jnp.dot(hot(early), full, preferred_element_type=jnp.float32)
    even = jnp.dot(hot(late), tail, preferred_element_type=jnp.float32)
    odd = jnp.dot(
        hot(jnp.where(late < 0, -1, late + 4)), tail, preferred_element_type=jnp.float32
    )
    for b, (group, gate, res) in enumerate(
        ((one, gate_one, res_one), (two, gate_two, res_two))
    ):
        r = slice(b * rows, (b + 1) * rows)
        for c in range(cols):
            s = slice(c * 128, (c + 1) * 128)
            h = slice(c // 2 * 128, (c // 2 + 1) * 128)
            answer = top[r, s] + (odd if c % 2 else even)[r, h]
            res[:, s] = (group[:, s].astype(jnp.float32) + gate[...] * answer).astype(BF)
        go(res, results[b], isem, False)
    for b, res in enumerate((res_one, res_two)):
        go(res, results[b], isem, True)

    @pl.when(i_move)
    def _():
        settled(stage, osem)


def shape(*dims, dtype=BF):
    return jax.ShapeDtypeStruct(dims, dtype)


def exchange(x):
    return lax.all_to_all(x, AXES, split_axis=0, concat_axis=0, tiled=True)


DMA = pltpu.SemaphoreType.DMA(())
SEMS = pltpu.SemaphoreType.DMA((GROUPS,))


def local(
    group_one, routes_one, gates_one, group_two, routes_two, gates_two,
    norm_gain, weight_in, weight_out, old_place, partner,
):
    rows, width = group_one.shape
    ff = weight_in.shape[2]
    me = lax.axis_index(AXES).astype(jnp.int32).reshape(1)
    w_in = tiles_of(weight_in, width, ff)
    w_out = tiles_of(weight_out, ff, width)
    buf1, pos, order = pl.pallas_call(
        first_kernel,
        out_shape=(
            shape(N, C1 + TOK, 8, 128),
            shape(2 * rows, 2, dtype=jnp.int32),
            shape(N, dtype=jnp.int32),
        ),
        in_specs=[SMEM, SMEM, HBM, HBM] + [HBM] * 6,
        out_specs=(HBM, HBM, SMEM),
        scratch_shapes=[
            pltpu.VMEM((N, C1 + TOK, 8, 128), BF),
            pltpu.VMEM((rows, width), BF), pltpu.VMEM((rows, width), BF),
            pltpu.VMEM((1, rows), jnp.int32), pltpu.VMEM((1, rows), jnp.int32),
            pltpu.VMEM((width // 128, 128), jnp.float32), pltpu.VMEM((1, N), jnp.int32),
            pltpu.VMEM((2 * rows, 2), jnp.int32), SEMS, DMA, DMA,
        ],
        name="first",
    )(
        me, partner, w_in, w_out, group_one, group_two,
        routes_one.reshape(1, rows), routes_two.reshape(1, rows),
        norm_gain.reshape(width // 128, 128), old_place.reshape(1, N),
    )
    recv1 = exchange(buf1)
    buf2 = pl.pallas_call(
        second_own_kernel,
        out_shape=shape(N, C2, 8, 128),
        in_specs=[SMEM, SMEM, SMEM, HBM, HBM],
        out_specs=HBM,
        scratch_shapes=[pltpu.VMEM((FEW, C2 + MA2, 8, 128), BF), DMA, DMA],
        name="second_own",
    )(me, partner, order, w_in, w_out)
    buf2 = pl.pallas_call(
        functools.partial(forward_kernel, (0, MA2, MB2), (0, 0, C2), False),
        out_shape=shape(N, C2, 8, 128),
        in_specs=[SMEM, SMEM, SMEM, HBM, HBM],
        out_specs=HBM,
        scratch_shapes=[pltpu.VMEM((N // 2, C2, 8, 128), BF), SEMS, DMA],
        input_output_aliases={4: 0},
        name="second_forward",
    )(me, partner, order, recv1, buf2)
    recv2 = exchange(buf2)
    arrived = recv1[:, C1:]
    cols = width // 128
    top = arrived[:, :cols].transpose(0, 2, 1, 3).reshape(N * 8, width)
    rest = arrived[:, cols:].reshape(N, cols // 2, 2, 4, 128)
    rest = rest.transpose(0, 3, 1, 2, 4).reshape(N * 4, width)
    inputs = jnp.concatenate([top, rest], axis=0)
    hidden = jnp.maximum(
        jnp.dot(inputs, weight_in[0], preferred_element_type=jnp.float32), 0.0
    ).astype(BF)
    result = jnp.dot(hidden, weight_out[0], preferred_element_type=jnp.float32).astype(BF)
    top = result[: N * 8].reshape(N, 8, cols, 128).transpose(0, 2, 1, 3)
    rest = result[N * 8 :].reshape(N, 4, cols // 2, 2, 128)
    rest = rest.transpose(0, 2, 3, 1, 4).reshape(N, cols // 2, 8, 128)
    answers = jnp.concatenate([top, rest], axis=1)
    buf3 = pl.pallas_call(
        functools.partial(forward_kernel, (MB2, 0, C1 - MB2), (C2, 0, C1 - C2), True),
        out_shape=shape(N, C3 + TOK, 8, 128),
        in_specs=[SMEM, SMEM, SMEM, HBM, HBM],
        out_specs=HBM,
        scratch_shapes=[
            pltpu.VMEM((N // 2, C1 - MB2, 8, 128), BF), pltpu.VMEM((N, TOK, 8, 128), BF),
            SEMS, DMA, DMA,
        ],
        name="third_held",
    )(me, partner, order, recv1, answers)
    buf3 = pl.pallas_call(
        functools.partial(forward_kernel, (0, C1 - MB2, MA2), (0, C1 - C2, C2), False),
        out_shape=shape(N, C3 + TOK, 8, 128),
        in_specs=[SMEM, SMEM, SMEM, HBM, HBM],
        out_specs=HBM,
        scratch_shapes=[pltpu.VMEM((N // 2, C2, 8, 128), BF), SEMS, DMA],
        input_output_aliases={4: 0},
        name="third_forward",
    )(me, partner, order, recv2, buf3)
    recv3 = exchange(buf3)
    new_in, new_out = pl.pallas_call(
        settle_kernel,
        out_shape=(shape(HALF, 8, 128), shape(HALF, 8, 128)),
        in_specs=[SMEM, SMEM, SMEM, HBM, HBM, HBM],
        out_specs=(HBM, HBM),
        scratch_shapes=[
            pltpu.VMEM((FEW, C2 + MB2, 8, 128), BF), pltpu.VMEM((HALF // 8, 8, 128), BF), DMA, DMA,
        ],
        name="settle",
    )(me, partner, order, w_in, w_out, recv2)
    res_one, res_two, new_in, new_out = pl.pallas_call(
        last_kernel,
        out_shape=(
            shape(rows, width), shape(rows, width), shape(HALF, 8, 128), shape(HALF, 8, 128),
        ),
        in_specs=[SMEM, SMEM, SMEM, HBM] + [HBM] * 7,
        out_specs=(HBM, HBM, HBM, HBM),
        scratch_shapes=[
            pltpu.VMEM((N, C3, 8, 128), BF), pltpu.VMEM((N, TOK, 8, 128), BF),
            pltpu.VMEM((2 * rows, 2), jnp.int32),
            pltpu.VMEM((rows, width), BF), pltpu.VMEM((rows, width), BF),
            pltpu.VMEM((rows, 1), jnp.float32), pltpu.VMEM((rows, 1), jnp.float32),
            pltpu.VMEM((rows, width), BF), pltpu.VMEM((rows, width), BF),
            SEMS, DMA, DMA, DMA,
        ],
        input_output_aliases={9: 2, 10: 3},
        name="last",
    )(
        me, partner, order, recv3, pos, group_one, group_two,
        gates_one.reshape(rows, 1), gates_two.reshape(rows, 1), new_in, new_out,
    )
    return (res_one, res_two, array_of(new_in, width, ff), array_of(new_out, ff, width))


def solution(mesh):
    split = P(AXES, None)
    flat = P(AXES)
    deep = P(AXES, None, None)
    return jax.shard_map(
        local,
        mesh=mesh,
        in_specs=(split, split, flat, split, split, flat, P(), deep, deep, P(), P()),
        out_specs=(split, split, deep, deep),
        check_vma=False,
    )
```

```python
import functools

import jax
import jax.numpy as jnp
from jax import lax
from jax.experimental import pallas as pl
from jax.experimental.pallas import tpu as pltpu
from jax.sharding import PartitionSpec as P

AXES = ("gx", "gy")
EPS = 1e-06
CAP = 6
N = 128
HALF = 2304
CHUNK = 72
TOK = 9
C1, C2, C3 = 21, 20, 21
NPART = 41
MA2 = 10
MB2 = C2 - MA2
GROUPS = 8
SIZE = N // GROUPS
UNROLL = 4

HBM = pl.BlockSpec(memory_space=pltpu.MemorySpace.HBM)
SMEM = pl.BlockSpec(memory_space=pltpu.SMEM)
VMEM = pl.BlockSpec(memory_space=pltpu.VMEM)
BF = jnp.bfloat16


def tiles_of(w, rows, cols):
    return w.reshape(rows // 8, 8, cols // 128, 128).transpose(0, 2, 1, 3).reshape(HALF, 8, 128)


def array_of(t, rows, cols):
    return t.reshape(rows // 8, cols // 128, 8, 128).transpose(0, 2, 1, 3).reshape(1, rows, cols)


def copies(partner, visit, after=None):
    def step(j, counts):
        movers, stayers = counts
        p = partner[j]
        moving = p != j
        visit(j, moving, jnp.where(moving, movers, stayers), p)
        one = moving.astype(jnp.int32)
        return (movers + one, stayers + 1 - one)

    def group(g, counts):
        counts = lax.fori_loop(g * SIZE, (g + 1) * SIZE, step, counts)
        if after is not None:
            after(g)
        return counts

    lax.fori_loop(0, GROUPS, group, (jnp.int32(0), jnp.int32(0)))


def own_piece(w_in, w_out, rank, offset, size, act):
    @pl.when(rank < 32)
    def _():
        act(w_in.at[pl.ds(rank * CHUNK + offset, size)])

    @pl.when(rank >= 32)
    def _():
        act(w_out.at[pl.ds((rank - 32) * CHUNK + offset, size)])


def go(src, dst, sem, wait):
    copy = pltpu.make_async_copy(src, dst, sem)
    if wait:
        copy.wait()
    else:
        copy.start()


def nothing(j, moving, rank, p):
    pass


def column(row):
    n = row.shape[1]
    eye = lax.broadcasted_iota(jnp.int32, (n, n), 0) == lax.broadcasted_iota(jnp.int32, (n, n), 1)
    return jnp.sum(jnp.where(eye, row, 0), axis=1, keepdims=True)


def both_halves(step, w_in, w_out):
    half = N // 4
    lax.fori_loop(0, half, lambda k, c: (step(k, w_in, k * CHUNK), c)[1], 0, unroll=UNROLL)
    lax.fori_loop(
        0, half, lambda k, c: (step(k + half, w_out, k * CHUNK), c)[1], 0, unroll=UNROLL
    )


def each_mover(step):
    lax.fori_loop(0, N // 2, lambda k, c: (step(k), c)[1], 0, unroll=UNROLL)


def settled(ref, sem):
    pltpu.make_async_copy(ref, ref, sem).wait()


def group_of(g):
    return pl.ds(g * SIZE, SIZE)


def first_kernel(
    me, partner, w_in, w_out, *refs,
):
    given, (buf1, pos_out, order, stage, *held, pos, sem, osem, isem) = refs[:6], refs[6:]
    one, two, routes_one, routes_two, gain, place = held
    my = me[0]
    i_move = partner[my] != my
    for src, dst in zip(given, held):
        go(src, dst, isem, False)

    def sort(j, counts):
        movers, stayers = counts
        moving = partner[j] != j
        order[jnp.where(moving, movers, stayers)] = j
        one = moving.astype(jnp.int32)
        return (movers + one, stayers + 1 - one)

    lax.fori_loop(0, N, sort, (jnp.int32(0), jnp.int32(N // 2)), unroll=UNROLL)

    @pl.when(i_move)
    def _():
        def step(k, w, tile):
            m = order[k]
            t = order[k + N // 2]
            go(w.at[pl.ds(tile, C1)], stage.at[t, pl.ds(0, C1)], sem.at[t // SIZE], False)
            go(w.at[pl.ds(tile + NPART, C1)], stage.at[m, pl.ds(0, C1)], sem.at[m // SIZE], False)

        both_halves(step, w_in, w_out)

    rows = one.shape[0]
    width = one.shape[1]
    cols = width // 128
    total = 2 * rows
    for src, dst in zip(given, held):
        go(src, dst, isem, True)
    slots = place[...]
    lower = (
        lax.broadcasted_iota(jnp.int32, (rows, rows), 1)
        < lax.broadcasted_iota(jnp.int32, (rows, rows), 0)
    ).astype(jnp.float32).astype(BF)
    lane = lax.broadcasted_iota(jnp.int32, (rows, N), 1)
    scale = jnp.concatenate([gain[c : c + 1, :] for c in range(cols)], axis=1)
    normed, target, place_in = [], [], []
    for b, (group, routes) in enumerate(((one, routes_one), (two, routes_two))):
        values = group[...].astype(jnp.float32)
        scaling = lax.rsqrt(jnp.mean(values * values, axis=1, keepdims=True) + EPS)
        normed.append((values * scaling * scale).astype(BF))
        member = column(routes[...]) == slots
        flag = member.astype(jnp.float32)
        before = jnp.dot(lower, flag.astype(BF), preferred_element_type=jnp.float32)
        target.append(jnp.sum(jnp.where(member, lane, 0), axis=1, keepdims=True))
        place_in.append(
            jnp.sum(flag * before, axis=1, keepdims=True).astype(jnp.int32) + b * CAP
        )
    normed = jnp.concatenate(normed, axis=0)
    target = jnp.concatenate(target, axis=0)
    place_in = jnp.concatenate(place_in, axis=0)
    early = jnp.where(place_in < 8, target * 8 + place_in, -1)
    late = jnp.where(place_in < 8, -1, target * 8 + place_in - 8)
    pos[:, 0:1] = early
    pos[:, 1:2] = late
    go(pos, pos_out, isem, False)

    def tiles(lo, size):
        go(stage.at[:, pl.ds(lo, size)], buf1.at[:, pl.ds(lo, size)], osem, False)

    def out(lo, size, g):
        part = group_of(g)
        go(stage.at[part, pl.ds(lo, size)], buf1.at[part, pl.ds(lo, size)], osem, False)

    @pl.when(i_move)
    def _():
        for g in range(GROUPS):
            settled(stage.at[group_of(g), pl.ds(0, C1)], sem.at[g])
            out(0, C1, g)

    eye = lax.broadcasted_iota(jnp.int32, (total, total), 0) == lax.broadcasted_iota(
        jnp.int32, (total, total), 1
    )
    early_row = jnp.sum(jnp.where(eye, early, 0), axis=0, keepdims=True)
    late_row = jnp.sum(jnp.where(eye, late, 0), axis=0, keepdims=True)
    row = lax.broadcasted_iota(jnp.int32, (N * 8, total), 0)
    fours = row - (row & 4)
    upper = lax.broadcasted_iota(jnp.int32, (N, 8, 128), 1) < 4
    cut = lambda x, c: x[:, c * 128 : (c + 1) * 128].reshape(N, 8, 128)
    pick = (fours == late_row).astype(jnp.float32).astype(BF)
    rest = jnp.dot(pick, normed, preferred_element_type=jnp.float32)
    for c in range(cols // 2):
        stage[:, C1 + cols + c] = jnp.where(upper, cut(rest, 2 * c), cut(rest, 2 * c + 1)).astype(BF)
    tiles(C1 + cols, cols // 2)
    pick = (row == early_row).astype(jnp.float32).astype(BF)
    top = jnp.dot(pick, normed, preferred_element_type=jnp.float32)
    for c in range(cols):
        stage[:, C1 + c] = cut(top, c).astype(BF)
    tiles(C1, cols)
    go(pos, pos_out, isem, True)
    settled(stage.at[:, pl.ds(C1, TOK)], osem)

    @pl.when(i_move)
    def _():
        settled(stage.at[:, pl.ds(0, C1)], osem)


def second_kernel(me, partner, order, w_in, w_out, recv1, buf2, stage, sem, osem):
    my = me[0]
    i_move = partner[my] != my

    @pl.when(i_move)
    def _():
        def step(k, w, tile):
            m = order[k]
            t = order[k + N // 2]
            at = sem.at[m // SIZE]
            go(w.at[pl.ds(tile + C1, C2)], stage.at[t], sem.at[t // SIZE], False)
            go(w.at[pl.ds(tile + NPART + C1, MA2)], stage.at[m, pl.ds(0, MA2)], at, False)
            go(recv1.at[partner[m], pl.ds(0, MB2)], stage.at[m, pl.ds(MA2, MB2)], at, False)

        both_halves(step, w_in, w_out)
        for g in range(GROUPS):
            settled(stage.at[group_of(g)], sem.at[g])
            go(stage.at[group_of(g)], buf2.at[group_of(g)], osem, False)
        settled(stage, osem)

    @pl.when(jnp.logical_not(i_move))
    def _():
        forward(order, partner, stage, buf2, sem, osem, C2, ((recv1, 0, 0, C2),))


def forward(order, partner, stage, buf, sem, osem, tiles, pieces, between=None):
    groups = N // 2 // SIZE

    def load(k):
        m = order[k]
        p = partner[m]
        for array, lo, to, size in pieces:
            go(array.at[p, pl.ds(lo, size)], stage.at[k, pl.ds(to, size)], sem.at[k // SIZE], False)

    each_mover(load)
    if between is not None:
        between()
    for g in range(groups):
        settled(stage.at[group_of(g), pl.ds(0, tiles)], sem.at[g])

        def send(i, c):
            k = g * SIZE + i
            go(stage.at[k, pl.ds(0, tiles)], buf.at[order[k], pl.ds(0, tiles)], osem, False)
            return c

        lax.fori_loop(0, SIZE, send, 0, unroll=UNROLL)
    settled(stage.at[pl.ds(0, N // 2), pl.ds(0, tiles)], osem)


def third_kernel(
    me, partner, order, recv1, recv2, answers, buf3, stage, tok, sem, osem, tsem
):
    my = me[0]
    i_move = partner[my] != my
    go(answers, tok, tsem, False)

    def tokens():
        go(answers, tok, tsem, True)
        go(tok, buf3.at[:, pl.ds(C3, TOK)], tsem, False)

    for mine, early, late in ((True, MB2, MA2), (False, C2, C2)):
        held = C1 - late

        @pl.when(i_move == mine)
        def _():
            forward(
                order, partner, stage, buf3, sem, osem, C3,
                ((recv1, early, 0, held), (recv2, 0, held, late)),
                tokens,
            )

    go(tok, buf3.at[:, pl.ds(C3, TOK)], tsem, True)


def settle_kernel(me, partner, w_in, w_out, recv2, new_in, new_out, stage, sem, osem):
    my = me[0]
    i_move = partner[my] != my

    def load(wait, g):
        part = pl.ds(g * SIZE * C2, SIZE * C2)
        go(recv2.at[part], stage.at[part], sem.at[g], wait)

    def visit(wait, j, moving, rank, p):
        if not wait:
            @pl.when(j % SIZE == 0)
            def _():
                load(True, j // SIZE)

        @pl.when(moving)
        def _():
            own_piece(
                new_in, new_out, rank, NPART, MB2,
                lambda dst: go(stage.at[pl.ds(j * C2 + MA2, MB2)], dst, osem, wait),
            )

        @pl.when(jnp.logical_not(moving))
        def _():
            own_piece(
                new_in, new_out, rank, 0, C2,
                lambda dst: go(stage.at[pl.ds(j * C2, C2)], dst, osem, wait),
            )

    @pl.when(i_move)
    def _():
        copies(partner, nothing, functools.partial(load, False))
        copies(partner, functools.partial(visit, False))
        copies(partner, functools.partial(visit, True))

    @pl.when(jnp.logical_not(i_move))
    def _():
        size = HALF // GROUPS
        pieces = [
            (src.at[pl.ds(g * size, size)], stage.at[pl.ds(h * HALF + g * size, size)],
             dst.at[pl.ds(g * size, size)], g)
            for h, (src, dst) in enumerate(((w_in, new_in), (w_out, new_out)))
            for g in range(GROUPS)
        ]
        for h in range(2):
            half = pieces[h * GROUPS : (h + 1) * GROUPS]
            for src, mid, dst, g in half:
                go(src, mid, sem.at[g], False)
            for src, mid, dst, g in half:
                go(src, mid, sem.at[g], True)
                go(mid, dst, osem, False)
        for src, mid, dst, g in pieces:
            go(mid, dst, osem, True)


def last_kernel(
    me, partner, order, recv3, *refs,
):
    given, (in_, out_, *results, new_in, new_out) = refs[:5], refs[5:11]
    stage, tok, *held, res_one, res_two, sem, osem, tsem, isem = refs[11:]
    pos, one, two, gate_one, gate_two = held
    my = me[0]
    i_move = partner[my] != my
    go(recv3.at[:, pl.ds(C3, TOK)], tok, tsem, False)

    def load(wait, g):
        part = group_of(g)
        go(recv3.at[part, pl.ds(0, C3)], stage.at[part], sem.at[g], wait)

    @pl.when(i_move)
    def _():
        for g in range(GROUPS):
            load(False, g)

    for src, dst in zip(given, held):
        go(src, dst, isem, False)
    rows = one.shape[0]
    width = one.shape[1]
    cols = width // 128
    total = 2 * rows
    for src, dst in zip(given, held):
        go(src, dst, isem, True)
    early = pos[:, 0:1]
    late = pos[:, 1:2]
    lane = lax.broadcasted_iota(jnp.int32, (total, N * 8), 1)
    hot = lambda where: (lane == where).astype(jnp.float32).astype(BF)

    @pl.when(i_move)
    def _():
        for g in range(GROUPS):
            load(True, g)

        def step(k, w, tile):
            go(stage.at[order[k + N // 2]], w.at[pl.ds(tile + C2, C3)], osem, False)
            go(stage.at[order[k]], w.at[pl.ds(tile + NPART + MB2, C3)], osem, False)

        both_halves(step, new_in, new_out)

    go(recv3.at[:, pl.ds(C3, TOK)], tok, tsem, True)
    flat = lambda c: tok[:, c].astype(jnp.float32).reshape(N * 8, 128).astype(BF)
    full = jnp.concatenate([flat(c) for c in range(cols)], axis=1)
    tail = jnp.concatenate([flat(cols + c) for c in range(cols // 2)], axis=1)
    top = jnp.dot(hot(early), full, preferred_element_type=jnp.float32)
    even = jnp.dot(hot(late), tail, preferred_element_type=jnp.float32)
    odd = jnp.dot(
        hot(jnp.where(late < 0, -1, late + 4)), tail, preferred_element_type=jnp.float32
    )
    for b, (group, gate, res) in enumerate(
        ((one, gate_one, res_one), (two, gate_two, res_two))
    ):
        r = slice(b * rows, (b + 1) * rows)
        for c in range(cols):
            s = slice(c * 128, (c + 1) * 128)
            h = slice(c // 2 * 128, (c // 2 + 1) * 128)
            answer = top[r, s] + (odd if c % 2 else even)[r, h]
            res[:, s] = (group[:, s].astype(jnp.float32) + gate[...] * answer).astype(BF)
        go(res, results[b], isem, False)
    for b, res in enumerate((res_one, res_two)):
        go(res, results[b], isem, True)

    @pl.when(i_move)
    def _():
        settled(stage, osem)


def shape(*dims, dtype=BF):
    return jax.ShapeDtypeStruct(dims, dtype)


def exchange(x):
    return lax.all_to_all(x, AXES, split_axis=0, concat_axis=0, tiled=True)


DMA = pltpu.SemaphoreType.DMA(())
SEMS = pltpu.SemaphoreType.DMA((GROUPS,))


def local(
    group_one, routes_one, gates_one, group_two, routes_two, gates_two,
    norm_gain, weight_in, weight_out, old_place, partner,
):
    rows, width = group_one.shape
    ff = weight_in.shape[2]
    me = lax.axis_index(AXES).astype(jnp.int32).reshape(1)
    w_in = tiles_of(weight_in, width, ff)
    w_out = tiles_of(weight_out, ff, width)
    buf1, pos, order = pl.pallas_call(
        first_kernel,
        out_shape=(
            shape(N, C1 + TOK, 8, 128),
            shape(2 * rows, 2, dtype=jnp.int32),
            shape(N, dtype=jnp.int32),
        ),
        in_specs=[SMEM, SMEM, HBM, HBM] + [HBM] * 6,
        out_specs=(HBM, HBM, SMEM),
        scratch_shapes=[
            pltpu.VMEM((N, C1 + TOK, 8, 128), BF),
            pltpu.VMEM((rows, width), BF), pltpu.VMEM((rows, width), BF),
            pltpu.VMEM((1, rows), jnp.int32), pltpu.VMEM((1, rows), jnp.int32),
            pltpu.VMEM((width // 128, 128), jnp.float32), pltpu.VMEM((1, N), jnp.int32),
            pltpu.VMEM((2 * rows, 2), jnp.int32), SEMS, DMA, DMA,
        ],
        name="first",
    )(
        me, partner, w_in, w_out, group_one, group_two,
        routes_one.reshape(1, rows), routes_two.reshape(1, rows),
        norm_gain.reshape(width // 128, 128), old_place.reshape(1, N),
    )
    recv1 = exchange(buf1)
    buf2 = pl.pallas_call(
        second_kernel,
        out_shape=shape(N, C2, 8, 128),
        in_specs=[SMEM, SMEM, SMEM, HBM, HBM, HBM],
        out_specs=HBM,
        scratch_shapes=[pltpu.VMEM((N, C2, 8, 128), BF), SEMS, DMA],
        name="second",
    )(me, partner, order, w_in, w_out, recv1)
    recv2 = exchange(buf2)
    arrived = recv1[:, C1:]
    cols = width // 128
    top = arrived[:, :cols].transpose(0, 2, 1, 3).reshape(N * 8, width)
    rest = arrived[:, cols:].reshape(N, cols // 2, 2, 4, 128)
    rest = rest.transpose(0, 3, 1, 2, 4).reshape(N * 4, width)
    inputs = jnp.concatenate([top, rest], axis=0)
    hidden = jnp.maximum(
        jnp.dot(inputs, weight_in[0], preferred_element_type=jnp.float32), 0.0
    ).astype(BF)
    result = jnp.dot(hidden, weight_out[0], preferred_element_type=jnp.float32).astype(BF)
    top = result[: N * 8].reshape(N, 8, cols, 128).transpose(0, 2, 1, 3)
    rest = result[N * 8 :].reshape(N, 4, cols // 2, 2, 128)
    rest = rest.transpose(0, 2, 3, 1, 4).reshape(N, cols // 2, 8, 128)
    answers = jnp.concatenate([top, rest], axis=1)
    buf3 = pl.pallas_call(
        third_kernel,
        out_shape=shape(N, C3 + TOK, 8, 128),
        in_specs=[SMEM, SMEM, SMEM, HBM, HBM, HBM],
        out_specs=HBM,
        scratch_shapes=[
            pltpu.VMEM((N // 2, C3, 8, 128), BF), pltpu.VMEM((N, TOK, 8, 128), BF), SEMS, DMA, DMA,
        ],
        name="third",
    )(me, partner, order, recv1, recv2, answers)
    recv3 = exchange(buf3)
    new_in, new_out = pl.pallas_call(
        settle_kernel,
        out_shape=(shape(HALF, 8, 128), shape(HALF, 8, 128)),
        in_specs=[SMEM, SMEM, HBM, HBM, HBM],
        out_specs=(HBM, HBM),
        scratch_shapes=[pltpu.VMEM((2 * HALF, 8, 128), BF), SEMS, DMA],
        name="settle",
    )(me, partner, w_in, w_out, recv2.reshape(N * C2, 8, 128))
    res_one, res_two, new_in, new_out = pl.pallas_call(
        last_kernel,
        out_shape=(
            shape(rows, width), shape(rows, width), shape(HALF, 8, 128), shape(HALF, 8, 128),
        ),
        in_specs=[SMEM, SMEM, SMEM, HBM] + [HBM] * 7,
        out_specs=(HBM, HBM, HBM, HBM),
        scratch_shapes=[
            pltpu.VMEM((N, C3, 8, 128), BF), pltpu.VMEM((N, TOK, 8, 128), BF),
            pltpu.VMEM((2 * rows, 2), jnp.int32),
            pltpu.VMEM((rows, width), BF), pltpu.VMEM((rows, width), BF),
            pltpu.VMEM((rows, 1), jnp.float32), pltpu.VMEM((rows, 1), jnp.float32),
            pltpu.VMEM((rows, width), BF), pltpu.VMEM((rows, width), BF),
            SEMS, DMA, DMA, DMA,
        ],
        input_output_aliases={9: 2, 10: 3},
        name="last",
    )(
        me, partner, order, recv3, pos, group_one, group_two,
        gates_one.reshape(rows, 1), gates_two.reshape(rows, 1), new_in, new_out,
    )
    return (res_one, res_two, array_of(new_in, width, ff), array_of(new_out, ff, width))


def solution(mesh):
    split = P(AXES, None)
    flat = P(AXES)
    deep = P(AXES, None, None)
    return jax.shard_map(
        local,
        mesh=mesh,
        in_specs=(split, split, flat, split, split, flat, P(), deep, deep, P(), P()),
        out_specs=(split, split, deep, deep),
        check_vma=False,
    )
```

```python
import functools

import jax
import jax.numpy as jnp
from jax import lax
from jax.experimental import pallas as pl
from jax.experimental.pallas import tpu as pltpu
from jax.sharding import PartitionSpec as P

AXES = ("gx", "gy")
EPS = 1e-06
CAP = 6
N = 128
HALF = 2304
CHUNK = 72
TOK = 9
C1, C2, C3 = 21, 20, 21
NPART = 41
MA2 = 10
MB2 = C2 - MA2
GROUPS = 4
SIZE = N // GROUPS
UNROLL = 4

HBM = pl.BlockSpec(memory_space=pltpu.MemorySpace.HBM)
SMEM = pl.BlockSpec(memory_space=pltpu.SMEM)
VMEM = pl.BlockSpec(memory_space=pltpu.VMEM)
BF = jnp.bfloat16


def tiles_of(w, rows, cols):
    return w.reshape(rows // 8, 8, cols // 128, 128).transpose(0, 2, 1, 3).reshape(HALF, 8, 128)


def array_of(t, rows, cols):
    return t.reshape(rows // 8, cols // 128, 8, 128).transpose(0, 2, 1, 3).reshape(1, rows, cols)


def copies(partner, visit, after=None):
    def step(j, counts):
        movers, stayers = counts
        p = partner[j]
        moving = p != j
        visit(j, moving, jnp.where(moving, movers, stayers), p)
        one = moving.astype(jnp.int32)
        return (movers + one, stayers + 1 - one)

    def group(g, counts):
        counts = lax.fori_loop(g * SIZE, (g + 1) * SIZE, step, counts)
        if after is not None:
            after(g)
        return counts

    lax.fori_loop(0, GROUPS, group, (jnp.int32(0), jnp.int32(0)))


def own_piece(w_in, w_out, rank, offset, size, act):
    @pl.when(rank < 32)
    def _():
        act(w_in.at[pl.ds(rank * CHUNK + offset, size)])

    @pl.when(rank >= 32)
    def _():
        act(w_out.at[pl.ds((rank - 32) * CHUNK + offset, size)])


def go(src, dst, sem, wait):
    copy = pltpu.make_async_copy(src, dst, sem)
    if wait:
        copy.wait()
    else:
        copy.start()


def nothing(j, moving, rank, p):
    pass


def column(row):
    n = row.shape[1]
    eye = lax.broadcasted_iota(jnp.int32, (n, n), 0) == lax.broadcasted_iota(jnp.int32, (n, n), 1)
    return jnp.sum(jnp.where(eye, row, 0), axis=1, keepdims=True)


def both_halves(step, w_in, w_out):
    half = N // 4
    lax.fori_loop(0, half, lambda k, c: (step(k, w_in, k * CHUNK), c)[1], 0, unroll=UNROLL)
    lax.fori_loop(
        0, half, lambda k, c: (step(k + half, w_out, k * CHUNK), c)[1], 0, unroll=UNROLL
    )


def each_mover(step):
    lax.fori_loop(0, N // 2, lambda k, c: (step(k), c)[1], 0, unroll=UNROLL)


def settled(ref, sem):
    pltpu.make_async_copy(ref, ref, sem).wait()


def group_of(g):
    return pl.ds(g * SIZE, SIZE)


def first_kernel(
    me, partner, w_in, w_out, *refs,
):
    given, (buf1, pos_out, order, stage, *held, pos, sem, osem, isem) = refs[:6], refs[6:]
    one, two, routes_one, routes_two, gain, place = held
    my = me[0]
    i_move = partner[my] != my
    for src, dst in zip(given, held):
        go(src, dst, isem, False)

    def sort(j, counts):
        movers, stayers = counts
        moving = partner[j] != j
        order[jnp.where(moving, movers, stayers)] = j
        one = moving.astype(jnp.int32)
        return (movers + one, stayers + 1 - one)

    lax.fori_loop(0, N, sort, (jnp.int32(0), jnp.int32(N // 2)), unroll=UNROLL)

    @pl.when(i_move)
    def _():
        def step(k, w, tile):
            m = order[k]
            t = order[k + N // 2]
            go(w.at[pl.ds(tile, C1)], stage.at[t, pl.ds(0, C1)], sem.at[t // SIZE], False)
            go(w.at[pl.ds(tile + NPART, C1)], stage.at[m, pl.ds(0, C1)], sem.at[m // SIZE], False)

        both_halves(step, w_in, w_out)

    rows = one.shape[0]
    width = one.shape[1]
    cols = width // 128
    total = 2 * rows
    for src, dst in zip(given, held):
        go(src, dst, isem, True)
    slots = place[...]
    lower = (
        lax.broadcasted_iota(jnp.int32, (rows, rows), 1)
        < lax.broadcasted_iota(jnp.int32, (rows, rows), 0)
    ).astype(jnp.float32).astype(BF)
    lane = lax.broadcasted_iota(jnp.int32, (rows, N), 1)
    scale = jnp.concatenate([gain[c : c + 1, :] for c in range(cols)], axis=1)
    normed, target, place_in = [], [], []
    for b, (group, routes) in enumerate(((one, routes_one), (two, routes_two))):
        values = group[...].astype(jnp.float32)
        scaling = lax.rsqrt(jnp.mean(values * values, axis=1, keepdims=True) + EPS)
        normed.append((values * scaling * scale).astype(BF))
        member = column(routes[...]) == slots
        flag = member.astype(jnp.float32)
        before = jnp.dot(lower, flag.astype(BF), preferred_element_type=jnp.float32)
        target.append(jnp.sum(jnp.where(member, lane, 0), axis=1, keepdims=True))
        place_in.append(
            jnp.sum(flag * before, axis=1, keepdims=True).astype(jnp.int32) + b * CAP
        )
    normed = jnp.concatenate(normed, axis=0)
    target = jnp.concatenate(target, axis=0)
    place_in = jnp.concatenate(place_in, axis=0)
    early = jnp.where(place_in < 8, target * 8 + place_in, -1)
    late = jnp.where(place_in < 8, -1, target * 8 + place_in - 8)
    pos[:, 0:1] = early
    pos[:, 1:2] = late
    go(pos, pos_out, isem, False)

    def tiles(lo, size):
        go(stage.at[:, pl.ds(lo, size)], buf1.at[:, pl.ds(lo, size)], osem, False)

    def out(lo, size, g):
        part = group_of(g)
        go(stage.at[part, pl.ds(lo, size)], buf1.at[part, pl.ds(lo, size)], osem, False)

    @pl.when(i_move)
    def _():
        for g in range(GROUPS):
            settled(stage.at[group_of(g), pl.ds(0, C1)], sem.at[g])
            out(0, C1, g)

    eye = lax.broadcasted_iota(jnp.int32, (total, total), 0) == lax.broadcasted_iota(
        jnp.int32, (total, total), 1
    )
    early_row = jnp.sum(jnp.where(eye, early, 0), axis=0, keepdims=True)
    late_row = jnp.sum(jnp.where(eye, late, 0), axis=0, keepdims=True)
    row = lax.broadcasted_iota(jnp.int32, (N * 8, total), 0)
    fours = row - (row & 4)
    upper = lax.broadcasted_iota(jnp.int32, (N, 8, 128), 1) < 4
    cut = lambda x, c: x[:, c * 128 : (c + 1) * 128].reshape(N, 8, 128)
    pick = (fours == late_row).astype(jnp.float32).astype(BF)
    rest = jnp.dot(pick, normed, preferred_element_type=jnp.float32)
    for c in range(cols // 2):
        stage[:, C1 + cols + c] = jnp.where(upper, cut(rest, 2 * c), cut(rest, 2 * c + 1)).astype(BF)
    tiles(C1 + cols, cols // 2)
    pick = (row == early_row).astype(jnp.float32).astype(BF)
    top = jnp.dot(pick, normed, preferred_element_type=jnp.float32)
    for c in range(cols):
        stage[:, C1 + c] = cut(top, c).astype(BF)
    tiles(C1, cols)
    go(pos, pos_out, isem, True)
    settled(stage.at[:, pl.ds(C1, TOK)], osem)

    @pl.when(i_move)
    def _():
        settled(stage.at[:, pl.ds(0, C1)], osem)


def second_kernel(me, partner, order, w_in, w_out, recv1, buf2, stage, sem, osem):
    my = me[0]
    i_move = partner[my] != my

    @pl.when(i_move)
    def _():
        def step(k, w, tile):
            m = order[k]
            t = order[k + N // 2]
            at = sem.at[m // SIZE]
            go(w.at[pl.ds(tile + C1, C2)], stage.at[t], sem.at[t // SIZE], False)
            go(w.at[pl.ds(tile + NPART + C1, MA2)], stage.at[m, pl.ds(0, MA2)], at, False)
            go(recv1.at[partner[m], pl.ds(0, MB2)], stage.at[m, pl.ds(MA2, MB2)], at, False)

        both_halves(step, w_in, w_out)
        for g in range(GROUPS):
            settled(stage.at[group_of(g)], sem.at[g])
            go(stage.at[group_of(g)], buf2.at[group_of(g)], osem, False)
        settled(stage, osem)

    @pl.when(jnp.logical_not(i_move))
    def _():
        forward(order, partner, stage, buf2, sem, osem, C2, ((recv1, 0, 0, C2),))


def forward(order, partner, stage, buf, sem, osem, tiles, pieces, between=None):
    groups = N // 2 // SIZE

    def load(k):
        m = order[k]
        p = partner[m]
        for array, lo, to, size in pieces:
            go(array.at[p, pl.ds(lo, size)], stage.at[k, pl.ds(to, size)], sem.at[k // SIZE], False)

    each_mover(load)
    if between is not None:
        between()
    for g in range(groups):
        settled(stage.at[group_of(g), pl.ds(0, tiles)], sem.at[g])

        def send(i, c):
            k = g * SIZE + i
            go(stage.at[k, pl.ds(0, tiles)], buf.at[order[k], pl.ds(0, tiles)], osem, False)
            return c

        lax.fori_loop(0, SIZE, send, 0, unroll=UNROLL)
    settled(stage.at[pl.ds(0, N // 2), pl.ds(0, tiles)], osem)


def third_kernel(
    me, partner, order, recv1, recv2, answers, buf3, stage, tok, sem, osem, tsem
):
    my = me[0]
    i_move = partner[my] != my
    go(answers, tok, tsem, False)

    def tokens():
        go(answers, tok, tsem, True)
        go(tok, buf3.at[:, pl.ds(C3, TOK)], tsem, False)

    for mine, early, late in ((True, MB2, MA2), (False, C2, C2)):
        held = C1 - late

        @pl.when(i_move == mine)
        def _():
            forward(
                order, partner, stage, buf3, sem, osem, C3,
                ((recv1, early, 0, held), (recv2, 0, held, late)),
                tokens,
            )

    go(tok, buf3.at[:, pl.ds(C3, TOK)], tsem, True)


def settle_kernel(me, partner, w_in, w_out, recv2, new_in, new_out, stage, sem, osem):
    my = me[0]
    i_move = partner[my] != my

    def load(wait, g):
        part = pl.ds(g * SIZE * C2, SIZE * C2)
        go(recv2.at[part], stage.at[part], sem.at[g], wait)

    def visit(wait, j, moving, rank, p):
        if not wait:
            @pl.when(j % SIZE == 0)
            def _():
                load(True, j // SIZE)

        @pl.when(moving)
        def _():
            own_piece(
                new_in, new_out, rank, NPART, MB2,
                lambda dst: go(stage.at[pl.ds(j * C2 + MA2, MB2)], dst, osem, wait),
            )

        @pl.when(jnp.logical_not(moving))
        def _():
            own_piece(
                new_in, new_out, rank, 0, C2,
                lambda dst: go(stage.at[pl.ds(j * C2, C2)], dst, osem, wait),
            )

    @pl.when(i_move)
    def _():
        copies(partner, nothing, functools.partial(load, False))
        copies(partner, functools.partial(visit, False))
        copies(partner, functools.partial(visit, True))

    @pl.when(jnp.logical_not(i_move))
    def _():
        size = HALF // GROUPS
        pieces = [
            (src.at[pl.ds(g * size, size)], stage.at[pl.ds(h * HALF + g * size, size)],
             dst.at[pl.ds(g * size, size)], g)
            for h, (src, dst) in enumerate(((w_in, new_in), (w_out, new_out)))
            for g in range(GROUPS)
        ]
        for h in range(2):
            half = pieces[h * GROUPS : (h + 1) * GROUPS]
            for src, mid, dst, g in half:
                go(src, mid, sem.at[g], False)
            for src, mid, dst, g in half:
                go(src, mid, sem.at[g], True)
                go(mid, dst, osem, False)
        for src, mid, dst, g in pieces:
            go(mid, dst, osem, True)


def last_kernel(
    me, partner, order, recv3, *refs,
):
    given, (in_, out_, *results, new_in, new_out) = refs[:5], refs[5:11]
    stage, tok, *held, res_one, res_two, sem, osem, tsem, isem = refs[11:]
    pos, one, two, gate_one, gate_two = held
    my = me[0]
    i_move = partner[my] != my
    go(recv3.at[:, pl.ds(C3, TOK)], tok, tsem, False)

    def load(wait, g):
        part = group_of(g)
        go(recv3.at[part, pl.ds(0, C3)], stage.at[part], sem.at[g], wait)

    @pl.when(i_move)
    def _():
        for g in range(GROUPS):
            load(False, g)

    for src, dst in zip(given, held):
        go(src, dst, isem, False)
    rows = one.shape[0]
    width = one.shape[1]
    cols = width // 128
    total = 2 * rows
    for src, dst in zip(given, held):
        go(src, dst, isem, True)
    early = pos[:, 0:1]
    late = pos[:, 1:2]
    lane = lax.broadcasted_iota(jnp.int32, (total, N * 8), 1)
    hot = lambda where: (lane == where).astype(jnp.float32).astype(BF)

    @pl.when(i_move)
    def _():
        for g in range(GROUPS):
            load(True, g)

        def step(k, w, tile):
            go(stage.at[order[k + N // 2]], w.at[pl.ds(tile + C2, C3)], osem, False)
            go(stage.at[order[k]], w.at[pl.ds(tile + NPART + MB2, C3)], osem, False)

        both_halves(step, new_in, new_out)

    go(recv3.at[:, pl.ds(C3, TOK)], tok, tsem, True)
    flat = lambda c: tok[:, c].astype(jnp.float32).reshape(N * 8, 128).astype(BF)
    full = jnp.concatenate([flat(c) for c in range(cols)], axis=1)
    tail = jnp.concatenate([flat(cols + c) for c in range(cols // 2)], axis=1)
    top = jnp.dot(hot(early), full, preferred_element_type=jnp.float32)
    even = jnp.dot(hot(late), tail, preferred_element_type=jnp.float32)
    odd = jnp.dot(
        hot(jnp.where(late < 0, -1, late + 4)), tail, preferred_element_type=jnp.float32
    )
    for b, (group, gate, res) in enumerate(
        ((one, gate_one, res_one), (two, gate_two, res_two))
    ):
        r = slice(b * rows, (b + 1) * rows)
        for c in range(cols):
            s = slice(c * 128, (c + 1) * 128)
            h = slice(c // 2 * 128, (c // 2 + 1) * 128)
            answer = top[r, s] + (odd if c % 2 else even)[r, h]
            res[:, s] = (group[:, s].astype(jnp.float32) + gate[...] * answer).astype(BF)
        go(res, results[b], isem, False)
    for b, res in enumerate((res_one, res_two)):
        go(res, results[b], isem, True)

    @pl.when(i_move)
    def _():
        settled(stage, osem)


def shape(*dims, dtype=BF):
    return jax.ShapeDtypeStruct(dims, dtype)


def exchange(x):
    return lax.all_to_all(x, AXES, split_axis=0, concat_axis=0, tiled=True)


DMA = pltpu.SemaphoreType.DMA(())
SEMS = pltpu.SemaphoreType.DMA((GROUPS,))


def local(
    group_one, routes_one, gates_one, group_two, routes_two, gates_two,
    norm_gain, weight_in, weight_out, old_place, partner,
):
    rows, width = group_one.shape
    ff = weight_in.shape[2]
    me = lax.axis_index(AXES).astype(jnp.int32).reshape(1)
    w_in = tiles_of(weight_in, width, ff)
    w_out = tiles_of(weight_out, ff, width)
    buf1, pos, order = pl.pallas_call(
        first_kernel,
        out_shape=(
            shape(N, C1 + TOK, 8, 128),
            shape(2 * rows, 2, dtype=jnp.int32),
            shape(N, dtype=jnp.int32),
        ),
        in_specs=[SMEM, SMEM, HBM, HBM] + [HBM] * 6,
        out_specs=(HBM, HBM, SMEM),
        scratch_shapes=[
            pltpu.VMEM((N, C1 + TOK, 8, 128), BF),
            pltpu.VMEM((rows, width), BF), pltpu.VMEM((rows, width), BF),
            pltpu.VMEM((1, rows), jnp.int32), pltpu.VMEM((1, rows), jnp.int32),
            pltpu.VMEM((width // 128, 128), jnp.float32), pltpu.VMEM((1, N), jnp.int32),
            pltpu.VMEM((2 * rows, 2), jnp.int32), SEMS, DMA, DMA,
        ],
        name="first",
    )(
        me, partner, w_in, w_out, group_one, group_two,
        routes_one.reshape(1, rows), routes_two.reshape(1, rows),
        norm_gain.reshape(width // 128, 128), old_place.reshape(1, N),
    )
    recv1 = exchange(buf1)
    buf2 = pl.pallas_call(
        second_kernel,
        out_shape=shape(N, C2, 8, 128),
        in_specs=[SMEM, SMEM, SMEM, HBM, HBM, HBM],
        out_specs=HBM,
        scratch_shapes=[pltpu.VMEM((N, C2, 8, 128), BF), SEMS, DMA],
        name="second",
    )(me, partner, order, w_in, w_out, recv1)
    recv2 = exchange(buf2)
    arrived = recv1[:, C1:]
    cols = width // 128
    top = arrived[:, :cols].transpose(0, 2, 1, 3).reshape(N * 8, width)
    rest = arrived[:, cols:].reshape(N, cols // 2, 2, 4, 128)
    rest = rest.transpose(0, 3, 1, 2, 4).reshape(N * 4, width)
    inputs = jnp.concatenate([top, rest], axis=0)
    hidden = jnp.maximum(
        jnp.dot(inputs, weight_in[0], preferred_element_type=jnp.float32), 0.0
    ).astype(BF)
    result = jnp.dot(hidden, weight_out[0], preferred_element_type=jnp.float32).astype(BF)
    top = result[: N * 8].reshape(N, 8, cols, 128).transpose(0, 2, 1, 3)
    rest = result[N * 8 :].reshape(N, 4, cols // 2, 2, 128)
    rest = rest.transpose(0, 2, 3, 1, 4).reshape(N, cols // 2, 8, 128)
    answers = jnp.concatenate([top, rest], axis=1)
    buf3 = pl.pallas_call(
        third_kernel,
        out_shape=shape(N, C3 + TOK, 8, 128),
        in_specs=[SMEM, SMEM, SMEM, HBM, HBM, HBM],
        out_specs=HBM,
        scratch_shapes=[
            pltpu.VMEM((N // 2, C3, 8, 128), BF), pltpu.VMEM((N, TOK, 8, 128), BF), SEMS, DMA, DMA,
        ],
        name="third",
    )(me, partner, order, recv1, recv2, answers)
    recv3 = exchange(buf3)
    new_in, new_out = pl.pallas_call(
        settle_kernel,
        out_shape=(shape(HALF, 8, 128), shape(HALF, 8, 128)),
        in_specs=[SMEM, SMEM, HBM, HBM, HBM],
        out_specs=(HBM, HBM),
        scratch_shapes=[pltpu.VMEM((2 * HALF, 8, 128), BF), SEMS, DMA],
        name="settle",
    )(me, partner, w_in, w_out, recv2.reshape(N * C2, 8, 128))
    res_one, res_two, new_in, new_out = pl.pallas_call(
        last_kernel,
        out_shape=(
            shape(rows, width), shape(rows, width), shape(HALF, 8, 128), shape(HALF, 8, 128),
        ),
        in_specs=[SMEM, SMEM, SMEM, HBM] + [HBM] * 7,
        out_specs=(HBM, HBM, HBM, HBM),
        scratch_shapes=[
            pltpu.VMEM((N, C3, 8, 128), BF), pltpu.VMEM((N, TOK, 8, 128), BF),
            pltpu.VMEM((2 * rows, 2), jnp.int32),
            pltpu.VMEM((rows, width), BF), pltpu.VMEM((rows, width), BF),
            pltpu.VMEM((rows, 1), jnp.float32), pltpu.VMEM((rows, 1), jnp.float32),
            pltpu.VMEM((rows, width), BF), pltpu.VMEM((rows, width), BF),
            SEMS, DMA, DMA, DMA,
        ],
        input_output_aliases={9: 2, 10: 3},
        name="last",
    )(
        me, partner, order, recv3, pos, group_one, group_two,
        gates_one.reshape(rows, 1), gates_two.reshape(rows, 1), new_in, new_out,
    )
    return (res_one, res_two, array_of(new_in, width, ff), array_of(new_out, ff, width))


def solution(mesh):
    split = P(AXES, None)
    flat = P(AXES)
    deep = P(AXES, None, None)
    return jax.shard_map(
        local,
        mesh=mesh,
        in_specs=(split, split, flat, split, split, flat, P(), deep, deep, P(), P()),
        out_specs=(split, split, deep, deep),
        check_vma=False,
    )
```
